32 devices in a mesh: rep: 8 (over y, x, core), exp: 4 (over z).
Axes of the slice: x: 2, y: 2, z: 4, core: 2. Of those that a mesh axis runs over, the one named last changes fastest.
Arguments:
- x_rows: bfloat16 [8, 512, 2048], P('rep', 'exp'), may hold values from -8 to 8
- row_cot: bfloat16 [8, 512, 2048], P('rep', 'exp'), may hold values from -8 to 8
- gate_vals: float32 [8, 512], P('rep', 'exp'), may hold values from 0 to 1, as said below
- route_pos: int32 [8, 80, 4], P('rep', 'exp'), may hold values from 0 to 115, as said below
- weights: bfloat16 [4, 3, 2048, 384], P('exp'), may hold values from -0.125 to 0.125
- momentum: float32 [4, 3, 2048, 384], P('exp', None, 'rep'), may hold values from -6 to 6
Outputs:
- token_grad: bfloat16 [8, 80, 2048], P('rep', 'exp')
- momentum_new: float32 [4, 3, 2048, 384], P('exp', None, 'rep')
The draws below stay inside these ranges and needn't reach their ends.
Inputs may be any that keep to these rules, and one draw needn't show every extreme that they name: `route_pos`: for each token of an owner, 4 positions e * 32 + c in ascending order, from 4 different experts e; from expert e an owner refers to slots c = 0 .. n - 1, each by exactly one token, where n is at most 20 and equals 20 for some expert of every owner; in every replica some owner uses all 20 slots of the last expert and some owner all of expert 0. `gate_vals`: row o * 32 + c of an expert in a replica belongs to owner o's slot c; its weight is zero exactly where no token of that owner refers to the slot, and positive elsewhere.
All inputs are finite; a program needn't handle non-finite values.
Results may differ from the reference program's by a relative error of at most 0.0064.
Values may be sent and summed in bfloat16 or wider, within the bound.
No kernel may reach another device: no remote copies, remote signals or barrier semaphores. Data moves between devices by JAX's collectives and lax.ppermute only.
A program may use at most 64 MiB of HBM per device.

```python
import math
import jax
import jax.numpy as jnp
from jax import lax

D = 2048
FF = 384
TOPK = 4
ROWS = 128
REPLICAS = 8
EXPERTS = 4
CAP = 32
TOK_DEV = 20
LIMIT = 20


def owner_routes(owner_key, full_expert):
    key_score, key_order = jax.random.split(owner_key, 2)
    raw_score = jax.random.randint(key_score, (EXPERTS, LIMIT), 0, 1 << 14)
    slot_index = jnp.arange(EXPERTS * LIMIT, dtype=jnp.int32).reshape(EXPERTS, LIMIT)
    expert_index = jnp.arange(EXPERTS, dtype=jnp.int32)
    scores = raw_score * (EXPERTS * LIMIT) + slot_index
    scores = jnp.where(expert_index[:, None] == full_expert, -1 - slot_index, scores)
    unused, chosen = lax.top_k(-scores.reshape(-1), TOK_DEV * TOPK)
    picked = jnp.zeros((EXPERTS * LIMIT,), jnp.int32).at[chosen].set(1)
    counts = jnp.sum(picked.reshape(EXPERTS, LIMIT), axis=1)
    ends = jnp.cumsum(counts)
    starts = ends - counts
    order_pos = jnp.arange(TOK_DEV * TOPK, dtype=jnp.int32)
    expert_of = jnp.sum((order_pos[:, None] >= ends[None, :]).astype(jnp.int32), axis=1)
    start_of = jnp.sum(jnp.where(expert_index[None, :] == expert_of[:, None], starts[None, :], 0), axis=1)
    positions = expert_of * CAP + (order_pos - start_of)
    by_token = positions.reshape(TOPK, TOK_DEV).T
    shuffle = jax.random.permutation(key_order, TOK_DEV)
    routes = jnp.zeros((TOK_DEV, TOPK), jnp.int32).at[shuffle].set(by_token)
    return (routes, counts)


def all_routes(key):
    base = jax.random.fold_in(key, 7)
    keys = jax.random.split(base, REPLICAS * EXPERTS)
    shifts = jax.random.randint(jax.random.fold_in(base, 13), (REPLICAS,), 0, EXPERTS)
    owners = jnp.arange(EXPERTS, dtype=jnp.int32)
    full_experts = ((owners[None, :] + shifts[:, None]) % EXPERTS).reshape(-1).astype(jnp.int32)
    routes, counts = jax.vmap(owner_routes)(keys, full_experts)
    return (routes.reshape(REPLICAS, EXPERTS * TOK_DEV, TOPK), counts.reshape(REPLICAS, EXPERTS, EXPERTS))


def draw_route_pos(key, part):
    return all_routes(key)[0].astype(jnp.int32)


def draw_gate_vals(key, part):
    unused, counts = all_routes(key)
    slots = jnp.arange(CAP, dtype=jnp.int32)
    by_expert = jnp.transpose(counts, (0, 2, 1))
    live = (slots[None, None, None, :] < by_expert[:, :, :, None]).astype(jnp.float32)
    value_key = jax.random.fold_in(key, 11)
    shape = (REPLICAS, EXPERTS, EXPERTS, CAP)
    values = jnp.exp(jax.random.uniform(value_key, shape, jnp.float32, math.log(0.1), 0.0))
    return (values * live).reshape(REPLICAS, EXPERTS * ROWS).astype(jnp.float32)


def mixed_rows(key, salt, amp_lo, with_signs):
    base = jax.random.fold_in(key, salt)
    key_scale, key_shared, key_own, key_amp, key_sign, key_pick = jax.random.split(base, 6)
    count_rows = EXPERTS * ROWS
    block_count = REPLICAS
    block_width = D // REPLICAS
    amp_sq = jax.random.uniform(key_amp, (block_count,), jnp.float32, amp_lo, 0.95)
    amp_shared = jnp.sqrt(amp_sq)
    amp_own = jnp.sqrt(1.0 - amp_sq)
    if with_signs:
        flip_block = jnp.where(jax.random.uniform(key_pick, (block_count,), jnp.float32) < 0.5, 1.0, 0.0)
        coin = jnp.where(jax.random.uniform(key_sign, (REPLICAS, block_count), jnp.float32) < 0.5, 1.0, -1.0)
        signs = 1.0 - flip_block[None, :] * (1.0 - coin)
    else:
        signs = jnp.ones((REPLICAS, block_count), jnp.float32)
    shared_weight = jnp.repeat(signs * amp_shared[None, :], block_width, axis=1)
    own_weight = jnp.repeat(amp_own, block_width, axis=0)
    col_scale = jnp.exp(jax.random.uniform(key_scale, (D,), jnp.float32, math.log(0.3), math.log(3.0)))
    shared = jax.random.normal(key_shared, (count_rows, D), jnp.float32)
    own_part = jax.random.normal(key_own, (REPLICAS, count_rows, D), jnp.float32)
    mixed = shared[None] * shared_weight[:, None, :] + own_part * own_weight[None, None, :]
    return jnp.clip(mixed * col_scale[None, None, :] / 1.4, -8.0, 8.0)


def draw_x_rows(key, part):
    return mixed_rows(key, 3, 0.5, False).astype(jnp.bfloat16)


def draw_row_cot(key, part):
    return mixed_rows(key, 5, 0.3, True).astype(jnp.bfloat16)


def block_levels(stream_key, extent, shards, least, top_value):
    gain, own = 1.0, jax.random.fold_in(stream_key, 6)
    for dim, shards_of in shards:
        steps = jnp.exp(jax.random.uniform(jax.random.fold_in(own, dim), (shards_of,), jnp.float32, least / len(shards), top_value / len(shards)))
        gain = gain * jnp.repeat(steps, extent[dim] // shards_of).reshape([-1 if axis == dim else 1 for axis in range(len(extent))])
    return gain


def gaussian(key, dims, width, reach, pieces=(), held_as=jnp.bfloat16):
    result = jax.random.normal(key, dims, jnp.float32) * width
    if len(pieces) > 0:
        result = block_levels(key, dims, pieces, -0.22, 0.18) * result
    return jnp.clip(result, min=-reach, max=reach).astype(held_as)


def setup_inputs(seed: int = 0) -> dict:
    arg_keys = jax.random.split(jax.random.key(seed), 7)
    x_rows = draw_x_rows(jax.random.fold_in(arg_keys[6], 71), 0)
    row_cot = draw_row_cot(jax.random.fold_in(arg_keys[6], 71), 0)
    gate_vals = draw_gate_vals(jax.random.fold_in(arg_keys[6], 71), 0)
    route_pos = draw_route_pos(jax.random.fold_in(arg_keys[6], 71), 0)
    weights = gaussian(arg_keys[4], (EXPERTS, 3, D, FF), D ** -0.5, 0.125, ((0, 4),))
    momentum = gaussian(arg_keys[5], (EXPERTS, 3, D, FF), 1.0, 6.0, ((0, 4), (2, 8)), jnp.float32)
    return dict(x_rows=x_rows, row_cot=row_cot, gate_vals=gate_vals, route_pos=route_pos, weights=weights, momentum=momentum)


tiny_eps = 1e-6
moment_decay = 0.9


def expert_backward(routed, out_cot, gate_row, w_gate, w_up, w_down_t):
    gate_pre = jnp.dot(routed, w_gate, preferred_element_type=jnp.float32)
    up_pre = jnp.dot(routed, w_up, preferred_element_type=jnp.float32)
    sigma_gate = jax.nn.sigmoid(gate_pre)
    activation = gate_pre * sigma_gate
    hidden = (activation * up_pre).astype(jnp.bfloat16)
    scaled = (gate_row[:, None] * out_cot.astype(jnp.float32)).astype(jnp.bfloat16)
    contract_rows = (((0,), (0,)), ((), ()))
    down_grad = lax.dot_general(scaled, hidden, contract_rows, preferred_element_type=jnp.float32)
    hidden_grad = jnp.dot(scaled, w_down_t, preferred_element_type=jnp.float32)
    gate_grad = (hidden_grad * up_pre * sigma_gate * (1.0 + gate_pre * (1.0 - sigma_gate))).astype(jnp.bfloat16)
    up_grad = (hidden_grad * activation).astype(jnp.bfloat16)
    contract_cols = (((1,), (1,)), ((), ()))
    row_grad = lax.dot_general(gate_grad, w_gate, contract_cols, preferred_element_type=jnp.float32)
    row_grad = row_grad + lax.dot_general(up_grad, w_up, contract_cols, preferred_element_type=jnp.float32)
    grad_gate = lax.dot_general(routed, gate_grad, contract_rows, preferred_element_type=jnp.float32)
    grad_up = lax.dot_general(routed, up_grad, contract_rows, preferred_element_type=jnp.float32)
    grad_stack = jnp.stack([grad_gate, grad_up, down_grad], axis=0).astype(jnp.bfloat16)
    return grad_stack, row_grad.astype(jnp.bfloat16)


def adasum_tree(grads):
    levels = REPLICAS.bit_length() - 1
    current = grads
    for section in range(levels):
        count = current.shape[0] // 2
        first_part = current[:count].astype(jnp.float32)
        second_part = current[count:].astype(jnp.float32)
        inner = jnp.sum(first_part * second_part, axis=(2, 3))
        first_sq = jnp.sum(first_part * first_part, axis=(2, 3))
        second_sq = jnp.sum(second_part * second_part, axis=(2, 3))
        coef_first = 1.0 - inner / (2.0 * (first_sq + tiny_eps))
        coef_second = 1.0 - inner / (2.0 * (second_sq + tiny_eps))
        merged = coef_first[:, :, None, None] * first_part + coef_second[:, :, None, None] * second_part
        if section == levels - 1:
            current = merged
        else:
            current = merged.astype(jnp.bfloat16)
    return current[0]


def reference(x_rows, row_cot, gate_vals, route_pos, weights, momentum):
    by_expert_x = x_rows.reshape(REPLICAS, EXPERTS, ROWS, D).transpose(1, 0, 2, 3)
    by_expert_c = row_cot.reshape(REPLICAS, EXPERTS, ROWS, D).transpose(1, 0, 2, 3)
    by_expert_g = gate_vals.reshape(REPLICAS, EXPERTS, ROWS).transpose(1, 0, 2)

    def per_expert(operands):
        xs_expert, cs_expert, gs_expert, w_expert = operands

        def per_replica(inner):
            return expert_backward(inner[0], inner[1], inner[2], w_expert[0], w_expert[1], w_expert[2])

        grads, row_grads = lax.map(per_replica, (xs_expert, cs_expert, gs_expert))
        return adasum_tree(grads), row_grads

    combined, row_grads = lax.map(per_expert, (by_expert_x, by_expert_c, by_expert_g, weights))
    received = row_grads.reshape(EXPERTS, REPLICAS, EXPERTS, CAP, D).transpose(1, 2, 0, 3, 4)
    received = received.reshape(REPLICAS, EXPERTS, EXPERTS * CAP, D)
    routes = route_pos.reshape(REPLICAS, EXPERTS, TOK_DEV, TOPK)

    def gather_owner(recv_rows, indices):
        return jnp.sum(recv_rows[indices].astype(jnp.float32), axis=1)

    def per_replica_tokens(operands):
        return jax.vmap(gather_owner)(operands[0], operands[1])

    tokens = lax.map(per_replica_tokens, (received, routes))
    token_grad = tokens.reshape(REPLICAS, EXPERTS * TOK_DEV, D).astype(jnp.bfloat16)
    momentum_new = moment_decay * momentum + (1.0 - moment_decay) * combined
    return token_grad, momentum_new
```

```python
import jax
import jax.numpy as jnp
from jax import lax
from jax.sharding import PartitionSpec as P

tiny_eps = 1e-06
moment_decay = 0.9
HIGHEST = lax.Precision.HIGHEST


def swap(block, axis, mask):
    count = lax.axis_size(axis)
    return lax.ppermute(block, axis, [(i, i ^ mask) for i in range(count)])


def live_rows(block, owners, live):
    width = block.shape[-1]
    return block.reshape(owners, -1, width)[:, :live].reshape(owners * live, width)


def adasum_weights(gram):
    count = gram.shape[-1]
    index = jnp.arange(count)
    weights = jnp.ones(gram.shape[:2], jnp.float32)
    half = count // 2
    while half >= 1:
        partner = index ^ half
        square = jnp.maximum(jnp.sum(jnp.where(index[:, None] == index[None, :], gram, 0.0), 2), 0.0)
        inner = jnp.sum(jnp.where(partner[:, None] == index[None, :], gram, 0.0), 2)
        bound = jnp.sqrt(square) * jnp.sqrt(square[:, partner])
        inner = jnp.clip(inner, -bound, bound)
        coef = 1.0 - inner / (2.0 * (square + tiny_eps))
        weights = weights * coef
        gram = gram * coef[:, :, None] * coef[:, None, :]
        gram = gram + gram[:, partner]
        gram = gram + gram[:, :, partner]
        half //= 2
    return weights


def on_device(x_rows, row_cot, gate_vals, route_pos, weights, momentum):
    reps = lax.axis_size("rep")
    experts = lax.axis_size("exp")
    me = lax.axis_index("rep")
    chip, core = me >> 1, me & 1
    chips = reps // 2
    cap = x_rows.shape[1] // experts
    live = min(cap, route_pos.shape[1])
    depth = x_rows.shape[2]
    width = depth // reps
    ff = weights.shape[3]
    contract_rows = (((0,), (0,)), ((), ()))
    contract_cols = (((1,), (1,)), ((), ()))

    routed = live_rows(x_rows[0], experts, live)
    out_cot = live_rows(row_cot[0], experts, live)
    gate_row = live_rows(gate_vals[0][:, None], experts, live)
    rows = routed.shape[0]
    w_gate, w_up, w_down_t = weights[0, 0], weights[0, 1], weights[0, 2]
    scaled = (gate_row * out_cot.astype(jnp.float32)).astype(jnp.bfloat16)
    gate_pre = jnp.dot(routed, w_gate, preferred_element_type=jnp.float32)
    up_pre = jnp.dot(routed, w_up, preferred_element_type=jnp.float32)
    sigma_gate = jax.nn.sigmoid(gate_pre)
    activation = gate_pre * sigma_gate
    hidden = (activation * up_pre).astype(jnp.bfloat16)
    hidden_grad = jnp.dot(scaled, w_down_t, preferred_element_type=jnp.float32)
    gate_grad = (hidden_grad * up_pre * sigma_gate * (1.0 + gate_pre * (1.0 - sigma_gate))).astype(
        jnp.bfloat16
    )
    up_grad = (hidden_grad * activation).astype(jnp.bfloat16)
    small = jnp.concatenate([gate_grad, up_grad, hidden], axis=1)

    pair = jnp.stack(
        [routed.reshape(rows, chips, 2, width), scaled.reshape(rows, chips, 2, width)], axis=3
    )
    pair = pair.transpose(1, 0, 2, 3, 4).reshape(chips, rows, 4 * width)
    tall, wide = [None] * reps, [None] * reps
    for step in range(chips):
        mine = lax.dynamic_index_in_dim(pair, chip ^ step, 0, keepdims=False)
        got_pair, got_small = mine, small
        if step:
            got_pair = swap(mine, "rep", 2 * step)
            got_small = swap(small, "rep", 2 * step)
        keep = lax.dynamic_slice_in_dim(got_pair, core * 2 * width, 2 * width, 1)
        give = lax.dynamic_slice_in_dim(got_pair, (1 - core) * 2 * width, 2 * width, 1)
        tall[2 * step], tall[2 * step + 1] = keep, swap(give, "rep", 1)
        wide[2 * step], wide[2 * step + 1] = got_small, swap(got_small, "rep", 1)
    tall = jnp.stack(tall)
    wide = jnp.stack(wide)
    lefts = [tall[:, :, :width], tall[:, :, :width], tall[:, :, width:]]
    rights = [wide[:, :, t * ff : (t + 1) * ff] for t in range(3)]

    row_grad = lax.dot_general(gate_grad, w_gate, contract_cols, preferred_element_type=jnp.float32)
    row_grad = row_grad + lax.dot_general(
        up_grad, w_up, contract_cols, preferred_element_type=jnp.float32
    )
    returned = lax.all_to_all(
        row_grad.astype(jnp.bfloat16), "exp", split_axis=0, concat_axis=0, tiled=True
    )
    place = route_pos[0] // cap * live + route_pos[0] % cap
    picks = jnp.sum(place[:, :, None] == jnp.arange(rows)[None, None, :], axis=1)
    token_grad = jnp.dot(
        picks.astype(jnp.bfloat16), returned, preferred_element_type=jnp.float32
    ).astype(jnp.bfloat16)[None]

    grams = []
    if reps * rows * rows <= width * ff:
        flat = reps * rows
        tall_gram = []
        for side in lefts[1:]:
            side = side.reshape(flat, width)
            tall_gram.append(
                lax.dot_general(side, side, contract_cols, preferred_element_type=jnp.float32)
            )
        for t in range(3):
            side = rights[t].reshape(flat, ff)
            wide_gram = lax.dot_general(
                side, side, contract_cols, preferred_element_type=jnp.float32
            )
            both = wide_gram * tall_gram[t // 2]
            grams.append(jnp.sum(both.reshape(reps, rows, reps, rows), axis=(1, 3)))
    else:
        for t in range(3):
            each = jnp.einsum(
                "rnd,rnf->rdf", lefts[t], rights[t], preferred_element_type=jnp.float32
            )
            grams.append(jnp.einsum("rdf,sdf->rs", each, each, precision=HIGHEST))
    gram = jnp.stack(grams)
    order = jnp.arange(reps) ^ me
    gram = gram[:, order][:, :, order]
    mask = reps // 2
    while mask >= 1:
        gram = gram + swap(gram, "rep", mask)
        mask //= 2
    coefs = adasum_weights(gram)[:, order]

    combined = []
    for t in range(3):
        right = (coefs[t][:, None, None] * rights[t].astype(jnp.float32)).astype(jnp.bfloat16)
        combined.append(
            lax.dot_general(
                lefts[t].reshape(reps * rows, width),
                right.reshape(reps * rows, ff),
                contract_rows,
                preferred_element_type=jnp.float32,
            )
        )
    combined = jnp.stack(combined)
    momentum_new = moment_decay * momentum + (1.0 - moment_decay) * combined[None]
    return (token_grad, momentum_new)


def solution(mesh):
    placed = (
        P("rep", "exp", None),
        P("rep", "exp", None),
        P("rep", "exp"),
        P("rep", "exp", None),
        P("exp", None, None, None),
        P("exp", None, "rep", None),
    )
    return jax.shard_map(
        on_device,
        mesh=mesh,
        in_specs=placed,
        out_specs=(P("rep", "exp", None), P("exp", None, "rep", None)),
        check_vma=False,
    )
```

```python
import functools

import jax
import jax.numpy as jnp
from jax import lax
from jax.experimental import pallas as pl
from jax.experimental.pallas import tpu as pltpu
from jax.sharding import PartitionSpec as P

tiny_eps = 1e-06
moment_decay = 0.9
HIGHEST = lax.Precision.HIGHEST
bf16, f32 = jnp.bfloat16, jnp.float32
contract_rows = (((0,), (0,)), ((), ()))
contract_cols = (((1,), (1,)), ((), ()))


def swap(block, axis, mask):
    count = lax.axis_size(axis)
    return lax.ppermute(block, axis, [(i, i ^ mask) for i in range(count)])


def live_rows(block, owners, live):
    width = block.shape[-1]
    return block.reshape(owners, -1, width)[:, :live].reshape(owners * live, width)


def backward_parts(gate_pre, up_pre, hidden_grad):
    sigma_gate = jax.nn.sigmoid(gate_pre)
    activation = gate_pre * sigma_gate
    hidden = (activation * up_pre).astype(bf16)
    gate_grad = (hidden_grad * up_pre * sigma_gate * (1.0 + gate_pre * (1.0 - sigma_gate))).astype(
        bf16
    )
    up_grad = (hidden_grad * activation).astype(bf16)
    return gate_grad, up_grad, hidden


def forward_kernel(sizes, chip_ref, x_ref, cot_ref, gate_ref, w_ref, *rest):
    owners, cap, live, chips, width, ff = sizes
    pair_refs, small_ref, acc = rest[:chips], rest[chips], rest[chips + 1]
    step = pl.program_id(0)
    slots, rows = owners * cap, owners * live
    row = lax.broadcasted_iota(jnp.int32, (rows, slots), 0)
    slot = lax.broadcasted_iota(jnp.int32, (rows, slots), 1)
    place = row
    for owner in range(1, owners):
        place = place + jnp.where(row >= owner * live, cap - live, 0)
    select = jnp.where(place == slot, 1.0, 0.0).astype(bf16)
    line = lax.broadcasted_iota(jnp.int32, (slots, slots), 0)
    lane = lax.broadcasted_iota(jnp.int32, (slots, slots), 1)
    gate = jnp.sum(jnp.where(line == lane, gate_ref[...], 0.0), axis=1, keepdims=True)
    scaled = (gate * cot_ref[0].astype(f32)).astype(bf16)
    routed = jnp.dot(select, x_ref[0], preferred_element_type=f32).astype(bf16)
    scaled = jnp.dot(select, scaled, preferred_element_type=f32).astype(bf16)
    parts = [
        jnp.dot(routed, w_ref[0, 0], preferred_element_type=f32),
        jnp.dot(routed, w_ref[0, 1], preferred_element_type=f32),
        jnp.dot(scaled, w_ref[0, 2], preferred_element_type=f32),
    ]

    @pl.when(step == 0)
    def _():
        for t in range(3):
            acc[t] = parts[t]

    @pl.when(step > 0)
    def _():
        for t in range(3):
            acc[t] += parts[t]

    for k in range(chips):

        @pl.when(step == k)
        def _():
            for core in range(2):
                at = core * 2 * width
                pair_refs[k][:, at : at + width] = routed[:, core * width : (core + 1) * width]
                pair_refs[k][:, at + width : at + 2 * width] = scaled[
                    :, core * width : (core + 1) * width
                ]

    @pl.when(step == chips - 1)
    def _():
        for t, part in enumerate(backward_parts(acc[0], acc[1], acc[2])):
            small_ref[:, t * ff : (t + 1) * ff] = part


def forward_call(x_rows, row_cot, gate_vals, weights, chip, sizes):
    owners, cap, live, chips, width, ff = sizes
    slots, rows = owners * cap, owners * live
    chunk = 2 * width
    grid_spec = pltpu.PrefetchScalarGridSpec(
        num_scalar_prefetch=1,
        grid=(chips,),
        in_specs=[
            pl.BlockSpec((1, slots, chunk), lambda k, c: (0, 0, c[0] ^ k)),
            pl.BlockSpec((1, slots, chunk), lambda k, c: (0, 0, c[0] ^ k)),
            pl.BlockSpec((1, slots), lambda k, c: (0, 0)),
            pl.BlockSpec((1, 3, chunk, ff), lambda k, c: (0, 0, c[0] ^ k, 0)),
        ],
        out_specs=[pl.BlockSpec((rows, 2 * chunk), lambda k, c: (0, 0))] * chips
        + [pl.BlockSpec((rows, 3 * ff), lambda k, c: (0, 0))],
        scratch_shapes=[pltpu.VMEM((3, rows, ff), f32)],
    )
    outs = pl.pallas_call(
        functools.partial(forward_kernel, sizes),
        out_shape=[jax.ShapeDtypeStruct((rows, 2 * chunk), bf16)] * chips
        + [jax.ShapeDtypeStruct((rows, 3 * ff), bf16)],
        grid_spec=grid_spec,
        cost_estimate=pl.CostEstimate(
            flops=6 * rows * chips * chunk * ff,
            bytes_accessed=weights.size * 2 + x_rows.size * 4,
            transcendentals=rows * ff,
        ),
        name="forward",
    )(chip.reshape(1), x_rows, row_cot, gate_vals, weights)
    return outs[:chips], outs[chips]


def tall_kernel(reps, width, *refs):
    tall_refs, gram_ref, flip_ref = refs[:reps], refs[reps], refs[reps + 1]
    for side in range(2):
        block = jnp.concatenate(
            [ref[:, side * width : (side + 1) * width] for ref in tall_refs], axis=0
        )
        gram_ref[side] = lax.dot_general(block, block, contract_cols, preferred_element_type=f32)
        flip_ref[side] = block.T


def tall_call(tall, width):
    reps, rows = len(tall), tall[0].shape[0]
    flat = reps * rows
    return pl.pallas_call(
        functools.partial(tall_kernel, reps, width),
        out_shape=[
            jax.ShapeDtypeStruct((2, flat, flat), f32),
            jax.ShapeDtypeStruct((2, width, flat), bf16),
        ],
        cost_estimate=pl.CostEstimate(
            flops=4 * flat * flat * width,
            bytes_accessed=8 * flat * flat + 8 * flat * width,
            transcendentals=0,
        ),
        name="tall",
    )(*tall)


def gram_kernel(reps, ff, me_ref, *refs):
    wide_refs, tall_ref, out_ref = refs[:reps], refs[reps], refs[reps + 1]
    rows = wide_refs[0].shape[0]
    flat = reps * rows
    me = me_ref[0]
    spot = lax.broadcasted_iota(jnp.int32, (flat, 128), 0)
    lane = lax.broadcasted_iota(jnp.int32, (flat, 128), 1)
    group = jnp.zeros_like(spot)
    for k in range(1, reps):
        group = group + jnp.where(spot >= k * rows, 1, 0)
    group = group ^ me
    gather = jnp.where(group == (lane & (reps - 1)), 1.0, 0.0)
    sums = []
    for t in range(3):
        block = jnp.concatenate([ref[:, t * ff : (t + 1) * ff] for ref in wide_refs], axis=0)
        both = lax.dot_general(block, block, contract_cols, preferred_element_type=f32)
        both = both * tall_ref[t // 2]
        sums.append(jnp.sum(both.reshape(reps, rows // 8, 8, flat), axis=1).reshape(reps * 8, flat))
    sums = jnp.dot(
        jnp.concatenate(sums, axis=0), gather, precision=HIGHEST, preferred_element_type=f32
    )
    sums = jnp.sum(sums.reshape(3 * reps, 8, 128), axis=1)
    for t in range(3):
        for k in range(reps):
            out_ref[pl.ds(t * reps + (me ^ k), 1), :] = sums[t * reps + k : t * reps + k + 1]


def gram_call(wide, tall_gram, me, ff):
    reps, rows = len(wide), wide[0].shape[0]
    flat = reps * rows
    vmem = pl.BlockSpec(memory_space=pltpu.VMEM)
    return pl.pallas_call(
        functools.partial(gram_kernel, reps, ff),
        out_shape=jax.ShapeDtypeStruct((3 * reps, 128), f32),
        in_specs=[pl.BlockSpec(memory_space=pltpu.SMEM)] + [vmem] * (reps + 1),
        out_specs=vmem,
        cost_estimate=pl.CostEstimate(
            flops=6 * flat * flat * ff,
            bytes_accessed=8 * flat * flat + 6 * flat * ff,
            transcendentals=0,
        ),
        name="gram",
    )(me.reshape(1), *wide, tall_gram)


def final_kernel(reps, ff, me_ref, gram_ref, flip_ref, *refs):
    wide_refs, moment_ref, out_ref, coef_ref = refs[:reps], refs[reps], refs[reps + 1], refs[reps + 2]
    me = me_ref[0]
    line = lax.broadcasted_iota(jnp.int32, (reps, 128), 0)
    lane = lax.broadcasted_iota(jnp.int32, (reps, 128), 1)
    near = lane & (reps - 1)
    for t in range(3):
        gram = gram_ref[t * reps : (t + 1) * reps, :]
        coefs = jnp.ones((reps, 128), f32)
        half = reps // 2
        while half >= 1:

            def factor(axis, spot):
                square = jnp.where(spot == line, gram, 0.0)
                square = jnp.maximum(jnp.sum(square, axis=axis, keepdims=True), 0.0)
                square = jnp.broadcast_to(square, (reps, 128))
                inner = jnp.where(spot == line ^ half, gram, 0.0)
                inner = jnp.sum(inner, axis=axis, keepdims=True)
                bound = jnp.sqrt(square * pltpu.roll(square, half, 1 - axis))
                inner = jnp.clip(inner, -bound, bound)
                return 1.0 - inner / (2.0 * (square + tiny_eps))

            by_line, by_lane = factor(1, lane), factor(0, near)
            coefs = coefs * by_line
            gram = gram * by_line * by_lane
            gram = gram + pltpu.roll(gram, half, 0)
            gram = gram + pltpu.roll(gram, half, 1)
            half //= 2
        coef_ref[t * reps : (t + 1) * reps, :] = jnp.concatenate([coefs] * (ff // 128), axis=1)
    for t in range(3):
        scaled = []
        for k in range(reps):
            coef = coef_ref[pl.ds(t * reps + (me ^ k), 1), :]
            scaled.append((coef * wide_refs[k][:, t * ff : (t + 1) * ff].astype(f32)).astype(bf16))
        combined = jnp.dot(
            flip_ref[t // 2], jnp.concatenate(scaled, axis=0), preferred_element_type=f32
        )
        out_ref[0, t] = moment_decay * moment_ref[0, t] + (1.0 - moment_decay) * combined


def final_call(gram, flip, wide, momentum, me, ff):
    reps, rows = len(wide), wide[0].shape[0]
    flat = reps * rows
    vmem = pl.BlockSpec(memory_space=pltpu.VMEM)
    return pl.pallas_call(
        functools.partial(final_kernel, reps, ff),
        out_shape=jax.ShapeDtypeStruct(momentum.shape, f32),
        in_specs=[pl.BlockSpec(memory_space=pltpu.SMEM)] + [vmem] * (reps + 3),
        out_specs=vmem,
        scratch_shapes=[pltpu.VMEM((3 * reps, ff), f32)],
        cost_estimate=pl.CostEstimate(
            flops=2 * flat * momentum.size,
            bytes_accessed=8 * momentum.size + 6 * flat * ff,
            transcendentals=0,
        ),
        name="final",
    )(me.reshape(1), gram, flip, *wide, momentum)


def adasum_weights(gram):
    count = gram.shape[-1]
    index = jnp.arange(count)
    weights = jnp.ones(gram.shape[:2], f32)
    half = count // 2
    while half >= 1:
        partner = index ^ half
        square = jnp.maximum(jnp.sum(jnp.where(index[:, None] == index[None, :], gram, 0.0), 2), 0.0)
        inner = jnp.sum(jnp.where(partner[:, None] == index[None, :], gram, 0.0), 2)
        bound = jnp.sqrt(square * square[:, partner])
        inner = jnp.clip(inner, -bound, bound)
        coef = 1.0 - inner / (2.0 * (square + tiny_eps))
        weights = weights * coef
        gram = gram * coef[:, :, None] * coef[:, None, :]
        gram = gram + gram[:, partner]
        gram = gram + gram[:, :, partner]
        half //= 2
    return weights


def forward_plain(x_rows, row_cot, gate_vals, weights, chip, sizes):
    owners, cap, live, chips, width, ff = sizes
    routed = live_rows(x_rows[0], owners, live)
    out_cot = live_rows(row_cot[0], owners, live)
    gate_row = live_rows(gate_vals[0][:, None], owners, live)
    rows = routed.shape[0]
    scaled = (gate_row * out_cot.astype(f32)).astype(bf16)
    gate_pre = jnp.dot(routed, weights[0, 0], preferred_element_type=f32)
    up_pre = jnp.dot(routed, weights[0, 1], preferred_element_type=f32)
    hidden_grad = jnp.dot(scaled, weights[0, 2], preferred_element_type=f32)
    small = jnp.concatenate(backward_parts(gate_pre, up_pre, hidden_grad), axis=1)
    pair = jnp.stack(
        [routed.reshape(rows, chips, 2, width), scaled.reshape(rows, chips, 2, width)], axis=3
    )
    pair = pair.transpose(1, 0, 2, 3, 4).reshape(chips, rows, 4 * width)
    pairs = [lax.dynamic_index_in_dim(pair, chip ^ k, 0, keepdims=False) for k in range(chips)]
    return pairs, small


def gram_plain(lefts, rights):
    grams = []
    for left, right in zip(lefts, rights, strict=True):
        each = jnp.einsum("rnd,rnf->rdf", left, right, preferred_element_type=f32)
        grams.append(jnp.einsum("rdf,sdf->rs", each, each, precision=HIGHEST))
    return jnp.stack(grams)


def final_plain(coefs, lefts, rights, momentum):
    combined = []
    for t in range(3):
        right = (coefs[t][:, None, None] * rights[t].astype(f32)).astype(bf16)
        left = lefts[t].reshape(-1, lefts[t].shape[2])
        combined.append(
            lax.dot_general(
                left, right.reshape(-1, right.shape[2]), contract_rows, preferred_element_type=f32
            )
        )
    return moment_decay * momentum + (1.0 - moment_decay) * jnp.stack(combined)[None]


def on_device(x_rows, row_cot, gate_vals, route_pos, weights, momentum):
    reps = lax.axis_size("rep")
    owners = lax.axis_size("exp")
    me = lax.axis_index("rep")
    chip, core = me >> 1, me & 1
    chips = reps // 2
    cap = x_rows.shape[1] // owners
    live = min(cap, route_pos.shape[1])
    rows = owners * live
    width = x_rows.shape[2] // reps
    ff = weights.shape[3]
    sizes = (owners, cap, live, chips, width, ff)
    with_kernels = width % 128 == 0 and ff % 128 == 0 and rows % 16 == 0 and reps == 8

    forward = forward_call if with_kernels else forward_plain
    pairs, small = forward(x_rows, row_cot, gate_vals, weights, chip, sizes)

    tall, wide = [None] * reps, [None] * reps
    for step in range(chips):
        got_pair = swap(pairs[step], "rep", 2 * step) if step else pairs[step]
        keep = lax.dynamic_slice_in_dim(got_pair, core * 2 * width, 2 * width, 1)
        give = lax.dynamic_slice_in_dim(got_pair, (1 - core) * 2 * width, 2 * width, 1)
        tall[2 * step], tall[2 * step + 1] = keep, swap(give, "rep", 1)
    for step in range(chips):
        got_small = swap(small, "rep", 2 * step) if step else small
        wide[2 * step], wide[2 * step + 1] = got_small, swap(got_small, "rep", 1)

    row_grad = lax.dot_general(
        small[:, :ff], weights[0, 0], contract_cols, preferred_element_type=f32
    )
    row_grad = row_grad + lax.dot_general(
        small[:, ff : 2 * ff], weights[0, 1], contract_cols, preferred_element_type=f32
    )
    returned = lax.all_to_all(
        row_grad.astype(bf16), "exp", split_axis=0, concat_axis=0, tiled=True
    )
    place = route_pos[0] // cap * live + route_pos[0] % cap
    picks = jnp.sum(place[:, :, None] == jnp.arange(rows)[None, None, :], axis=1)
    token_grad = jnp.dot(picks.astype(bf16), returned, preferred_element_type=f32)
    token_grad = token_grad.astype(bf16)[None]

    if with_kernels:
        tall_gram, flip = tall_call(tall, width)
        gram = gram_call(wide, tall_gram, me, ff)
    else:
        tall, wide = jnp.stack(tall), jnp.stack(wide)
        lefts = [tall[:, :, :width], tall[:, :, :width], tall[:, :, width:]]
        rights = [wide[:, :, t * ff : (t + 1) * ff] for t in range(3)]
        order = jnp.arange(reps) ^ me
        gram = gram_plain(lefts, rights)[:, order][:, :, order]
    mask = reps // 2
    while mask >= 1:
        gram = gram + swap(gram, "rep", mask)
        mask //= 2
    if with_kernels:
        momentum_new = final_call(gram, flip, wide, momentum, me, ff)
    else:
        momentum_new = final_plain(adasum_weights(gram)[:, order], lefts, rights, momentum)
    return (token_grad, momentum_new)


def solution(mesh):
    placed = (
        P("rep", "exp", None),
        P("rep", "exp", None),
        P("rep", "exp"),
        P("rep", "exp", None),
        P("exp", None, None, None),
        P("exp", None, "rep", None),
    )
    return jax.shard_map(
        on_device,
        mesh=mesh,
        in_specs=placed,
        out_specs=(P("rep", "exp", None), P("exp", None, "rep", None)),
        check_vma=False,
    )
```

```python
import functools

import jax
import jax.numpy as jnp
from jax import lax
from jax.experimental import pallas as pl
from jax.experimental.pallas import tpu as pltpu
from jax.sharding import PartitionSpec as P

tiny_eps = 1e-06
moment_decay = 0.9
HIGHEST = lax.Precision.HIGHEST
bf16, f32 = jnp.bfloat16, jnp.float32
contract_rows = (((0,), (0,)), ((), ()))
contract_cols = (((1,), (1,)), ((), ()))


def swap(block, axis, mask):
    count = lax.axis_size(axis)
    return lax.ppermute(block, axis, [(i, i ^ mask) for i in range(count)])


def live_rows(block, owners, live):
    width = block.shape[-1]
    return block.reshape(owners, -1, width)[:, :live].reshape(owners * live, width)


def backward_parts(gate_pre, up_pre, hidden_grad):
    sigma_gate = jax.nn.sigmoid(gate_pre)
    activation = gate_pre * sigma_gate
    hidden = (activation * up_pre).astype(bf16)
    gate_grad = (hidden_grad * up_pre * sigma_gate * (1.0 + gate_pre * (1.0 - sigma_gate))).astype(
        bf16
    )
    up_grad = (hidden_grad * activation).astype(bf16)
    return gate_grad, up_grad, hidden


VMEM = pl.BlockSpec(memory_space=pltpu.VMEM)


def kernel_params(mib):
    return pltpu.CompilerParams(vmem_limit_bytes=mib << 20)


def spread_rows(index, live, cap, owners):
    place = index
    for owner in range(1, owners):
        place = place + jnp.where(index >= owner * live, cap - live, 0)
    return place


def pack_kernel(sizes, x_ref, cot_ref, gate_ref, *out_refs):
    owners, cap, live, chips, width, ff = sizes
    slots, rows = owners * cap, owners * live
    chip = lax.axis_index("rep") >> 1
    place = spread_rows(lax.broadcasted_iota(jnp.int32, (rows, slots), 0), live, cap, owners)
    slot = lax.broadcasted_iota(jnp.int32, (rows, slots), 1)
    select = jnp.where(place == slot, 1.0, 0.0).astype(bf16)
    line = lax.broadcasted_iota(jnp.int32, (slots, slots), 0)
    lane = lax.broadcasted_iota(jnp.int32, (slots, slots), 1)
    gate = jnp.sum(jnp.where(line == lane, gate_ref[...], 0.0), axis=1, keepdims=True)
    for k in range(chips):
        at = pl.ds(pl.multiple_of((chip ^ k) * 2 * width, 2 * width), 2 * width)
        scaled = (gate * cot_ref[0, :, at].astype(f32)).astype(bf16)
        routed = jnp.dot(select, x_ref[0, :, at], preferred_element_type=f32).astype(bf16)
        scaled = jnp.dot(select, scaled, preferred_element_type=f32).astype(bf16)
        for core in range(2):
            out_refs[k][core, :, :width] = routed[:, core * width : (core + 1) * width]
            out_refs[k][core, :, width:] = scaled[:, core * width : (core + 1) * width]


def pack_call(x_rows, row_cot, gate_vals, sizes):
    owners, cap, live, chips, width, ff = sizes
    rows = owners * live
    return pl.pallas_call(
        functools.partial(pack_kernel, sizes),
        out_shape=[jax.ShapeDtypeStruct((2, rows, 2 * width), bf16)] * chips,
        in_specs=[VMEM] * 3,
        out_specs=[VMEM] * chips,
        compiler_params=kernel_params(6),
        cost_estimate=pl.CostEstimate(
            flops=4 * rows * x_rows.size, bytes_accessed=8 * x_rows.size, transcendentals=0
        ),
        name="pack",
    )(x_rows, row_cot, gate_vals)


def forward_kernel(sizes, *refs):
    owners, cap, live, chips, width, ff = sizes
    pair_refs, w_ref, small_ref = refs[:chips], refs[chips], refs[chips + 1]
    chip = lax.axis_index("rep") >> 1
    sums = [None] * 3
    for k in range(chips):
        for core in range(2):
            at = pl.ds(pl.multiple_of(((chip ^ k) * 2 + core) * width, width), width)
            for t in range(3):
                left = pair_refs[k][core, :, width:] if t == 2 else pair_refs[k][core, :, :width]
                part = jnp.dot(left, w_ref[0, t, at, :], preferred_element_type=f32)
                sums[t] = part if sums[t] is None else sums[t] + part
    for t, part in enumerate(backward_parts(*sums)):
        small_ref[:, t * ff : (t + 1) * ff] = part


def forward_call(pairs, weights, sizes):
    owners, cap, live, chips, width, ff = sizes
    rows = owners * live
    return pl.pallas_call(
        functools.partial(forward_kernel, sizes),
        out_shape=jax.ShapeDtypeStruct((rows, 3 * ff), bf16),
        in_specs=[VMEM] * (chips + 1),
        out_specs=VMEM,
        compiler_params=kernel_params(7),
        cost_estimate=pl.CostEstimate(
            flops=2 * rows * weights.size,
            bytes_accessed=2 * weights.size,
            transcendentals=rows * ff,
        ),
        name="forward",
    )(*pairs, weights)


def back_kernel(sizes, small_ref, w_ref, *out_refs):
    owners, cap, live, chips, width, ff = sizes
    slots, rows = owners * cap, owners * live
    me = lax.axis_index("exp")
    slot = lax.broadcasted_iota(jnp.int32, (slots, rows), 0)
    row = lax.broadcasted_iota(jnp.int32, (slots, rows), 1)
    place = jnp.full((slots, rows), -1, jnp.int32)
    for k in range(owners):
        inside = (slot >= k * cap) & (slot < k * cap + live)
        place = jnp.where(inside, slot - k * cap + (me ^ k) * live, place)
    select = jnp.where(place == row, 1.0, 0.0).astype(bf16)
    spread = jnp.dot(select, small_ref[:, : 2 * ff], preferred_element_type=f32).astype(bf16)
    chunk = 2 * width
    for c in range(chips):
        at = slice(c * chunk, (c + 1) * chunk)
        grad = lax.dot_general(
            spread[:, :ff], w_ref[0, 0, at, :], contract_cols, preferred_element_type=f32
        ) + lax.dot_general(
            spread[:, ff:], w_ref[0, 1, at, :], contract_cols, preferred_element_type=f32
        )
        grad = grad.astype(bf16)
        for k in range(owners):
            out_refs[k][:, at] = grad[k * cap : k * cap + live]


def back_call(small, weights, sizes):
    owners, cap, live, chips, width, ff = sizes
    rows, depth = owners * live, weights.shape[2]
    return pl.pallas_call(
        functools.partial(back_kernel, sizes),
        out_shape=[jax.ShapeDtypeStruct((live, depth), bf16)] * owners,
        in_specs=[VMEM] * 2,
        out_specs=[VMEM] * owners,
        compiler_params=kernel_params(7),
        cost_estimate=pl.CostEstimate(
            flops=4 * rows * depth * ff,
            bytes_accessed=weights.size * 4 // 3,
            transcendentals=0,
        ),
        name="back",
    )(small, weights)


def token_kernel(cap, route_ref, *refs):
    row_refs, out_ref, held = refs[:-2], refs[-2], refs[-1]
    owners, live = len(row_refs), row_refs[0].shape[0]
    me = lax.axis_index("exp")
    held[...] = jnp.zeros_like(held)
    for k in range(owners):
        held[k * cap : k * cap + live] = row_refs[k][...]
    picks, tokens = route_ref.shape[1:]
    line = lax.broadcasted_iota(jnp.int32, (owners * cap, tokens), 0)
    place = line
    for k in range(owners):
        inside = (line >= k * cap) & (line < (k + 1) * cap)
        place = jnp.where(inside, line + ((me ^ k) - k) * cap, place)
    choice = jnp.zeros((owners * cap, tokens), f32)
    for pick in range(picks):
        choice = choice + jnp.where(route_ref[0, pick : pick + 1, :] == place, 1.0, 0.0)
    sums = lax.dot_general(
        choice.astype(bf16), held[...], contract_rows, preferred_element_type=f32
    )
    out_ref[0] = sums.astype(bf16)


def token_call(route_pos, returned, cap):
    owners, (live, depth) = len(returned), returned[0].shape
    return pl.pallas_call(
        functools.partial(token_kernel, cap),
        out_shape=jax.ShapeDtypeStruct((1, route_pos.shape[1], depth), bf16),
        in_specs=[VMEM] * (owners + 1),
        out_specs=VMEM,
        scratch_shapes=[pltpu.VMEM((owners * cap, depth), bf16)],
        compiler_params=kernel_params(6),
        cost_estimate=pl.CostEstimate(
            flops=2 * route_pos.shape[1] * owners * cap * depth,
            bytes_accessed=owners * live * depth * 4,
            transcendentals=0,
        ),
        name="token",
    )(route_pos.swapaxes(1, 2), *returned)


def tall_kernel(reps, *refs):
    tall_refs, gram_ref, flip_ref = refs[:reps], refs[reps], refs[reps + 1]
    width = tall_refs[0].shape[2] // 2
    core = lax.axis_index("rep") & 1
    for side in range(2):
        at = slice(side * width, (side + 1) * width)
        both = jnp.concatenate(
            [jnp.concatenate([ref[0, :, at], ref[1, :, at]], axis=1) for ref in tall_refs], axis=0
        )
        gram_ref[side] = lax.dot_general(both, both, contract_cols, preferred_element_type=f32)
        own = jnp.concatenate([ref[core, :, at] for ref in tall_refs], axis=0)
        flip_ref[side] = own.T


def tall_call(tall):
    reps, (cores, rows, width) = len(tall), tall[0].shape
    width //= 2
    flat = reps * rows
    return pl.pallas_call(
        functools.partial(tall_kernel, reps),
        out_shape=[
            jax.ShapeDtypeStruct((2, flat, flat), f32),
            jax.ShapeDtypeStruct((2, width, flat), bf16),
        ],
        in_specs=[VMEM] * reps,
        out_specs=[VMEM] * 2,
        compiler_params=kernel_params(6),
        cost_estimate=pl.CostEstimate(
            flops=8 * flat * flat * width,
            bytes_accessed=8 * flat * flat + 12 * flat * width,
            transcendentals=0,
        ),
        name="tall",
    )(*tall)


def gram_kernel(reps, ff, *refs):
    wide_refs, tall_ref, out_ref = refs[:reps], refs[reps], refs[reps + 1]
    rows = wide_refs[0].shape[0]
    flat = reps * rows
    me = lax.axis_index("rep")
    spot = lax.broadcasted_iota(jnp.int32, (flat, 128), 0)
    lane = lax.broadcasted_iota(jnp.int32, (flat, 128), 1)
    group = jnp.zeros_like(spot)
    for k in range(1, reps):
        group = group + jnp.where(spot >= k * rows, 1, 0)
    gather = jnp.where((group ^ me) == (lane & (reps - 1)), 1.0, 0.0)
    sums = []
    for t in range(3):
        block = jnp.concatenate([ref[:, t * ff : (t + 1) * ff] for ref in wide_refs], axis=0)
        both = lax.dot_general(block, block, contract_cols, preferred_element_type=f32)
        both = both * tall_ref[t // 2]
        sums.append(jnp.sum(both.reshape(reps, rows // 8, 8, flat), axis=1).reshape(reps * 8, flat))
    sums = jnp.dot(
        jnp.concatenate(sums, axis=0), gather, precision=HIGHEST, preferred_element_type=f32
    )
    sums = jnp.sum(sums.reshape(3 * reps, 8, 128), axis=1)
    for t in range(3):
        for k in range(reps):
            out_ref[pl.ds(t * reps + (me ^ k), 1), :] = sums[t * reps + k : t * reps + k + 1]


def gram_call(wide, tall_gram, ff):
    reps, rows = len(wide), wide[0].shape[0]
    flat = reps * rows
    return pl.pallas_call(
        functools.partial(gram_kernel, reps, ff),
        out_shape=jax.ShapeDtypeStruct((3 * reps, 128), f32),
        in_specs=[VMEM] * (reps + 1),
        out_specs=VMEM,
        compiler_params=kernel_params(6),
        cost_estimate=pl.CostEstimate(
            flops=6 * flat * flat * ff,
            bytes_accessed=8 * flat * flat + 6 * flat * ff,
            transcendentals=0,
        ),
        name="gram",
    )(*wide, tall_gram)


def final_kernel(reps, ff, gram_ref, other_ref, flip_ref, *refs):
    wide_refs, moment_ref, out_ref, coef_ref = refs[:reps], refs[reps], refs[reps + 1], refs[reps + 2]
    me = lax.axis_index("rep")
    line = lax.broadcasted_iota(jnp.int32, (reps, 128), 0)
    lane = lax.broadcasted_iota(jnp.int32, (reps, 128), 1)
    near = lane & (reps - 1)
    for t in range(3):
        part = slice(t * reps, (t + 1) * reps)
        gram = gram_ref[part, :] + other_ref[part, :]
        coefs = jnp.ones((reps, 128), f32)
        half = reps // 2
        while half >= 1:

            def factor(axis, spot):
                square = jnp.where(spot == line, gram, 0.0)
                square = jnp.maximum(jnp.sum(square, axis=axis, keepdims=True), 0.0)
                square = jnp.broadcast_to(square, (reps, 128))
                inner = jnp.where(spot == line ^ half, gram, 0.0)
                inner = jnp.sum(inner, axis=axis, keepdims=True)
                bound = jnp.sqrt(square * pltpu.roll(square, half, 1 - axis))
                inner = jnp.clip(inner, -bound, bound)
                return 1.0 - inner / (2.0 * (square + tiny_eps))

            by_line, by_lane = factor(1, lane), factor(0, near)
            coefs = coefs * by_line
            gram = gram * by_line * by_lane
            gram = gram + pltpu.roll(gram, half, 0)
            gram = gram + pltpu.roll(gram, half, 1)
            half //= 2
        coef_ref[part, :] = jnp.concatenate([coefs] * (ff // 128), axis=1)
    for t in range(3):
        scaled = []
        for k in range(reps):
            coef = coef_ref[pl.ds(t * reps + (me ^ k), 1), :]
            scaled.append((coef * wide_refs[k][:, t * ff : (t + 1) * ff].astype(f32)).astype(bf16))
        combined = jnp.dot(
            flip_ref[t // 2], jnp.concatenate(scaled, axis=0), preferred_element_type=f32
        )
        out_ref[0, t] = moment_decay * moment_ref[0, t] + (1.0 - moment_decay) * combined


def final_call(gram, other, flip, wide, momentum, ff):
    reps, rows = len(wide), wide[0].shape[0]
    return pl.pallas_call(
        functools.partial(final_kernel, reps, ff),
        out_shape=jax.ShapeDtypeStruct(momentum.shape, f32),
        in_specs=[VMEM] * (reps + 4),
        out_specs=VMEM,
        scratch_shapes=[pltpu.VMEM((3 * reps, ff), f32)],
        compiler_params=kernel_params(6),
        cost_estimate=pl.CostEstimate(
            flops=2 * reps * rows * momentum.size,
            bytes_accessed=8 * momentum.size + 6 * reps * rows * ff,
            transcendentals=0,
        ),
        name="final",
    )(gram, other, flip, *wide, momentum)


def adasum_weights(gram):
    count = gram.shape[-1]
    index = jnp.arange(count)
    weights = jnp.ones(gram.shape[:2], f32)
    half = count // 2
    while half >= 1:
        partner = index ^ half
        square = jnp.maximum(jnp.sum(jnp.where(index[:, None] == index[None, :], gram, 0.0), 2), 0.0)
        inner = jnp.sum(jnp.where(partner[:, None] == index[None, :], gram, 0.0), 2)
        bound = jnp.sqrt(square * square[:, partner])
        inner = jnp.clip(inner, -bound, bound)
        coef = 1.0 - inner / (2.0 * (square + tiny_eps))
        weights = weights * coef
        gram = gram * coef[:, :, None] * coef[:, None, :]
        gram = gram + gram[:, partner]
        gram = gram + gram[:, :, partner]
        half //= 2
    return weights


def forward_plain(x_rows, row_cot, gate_vals, weights, sizes):
    owners, cap, live, chips, width, ff = sizes
    routed = live_rows(x_rows[0], owners, live)
    out_cot = live_rows(row_cot[0], owners, live)
    gate_row = live_rows(gate_vals[0][:, None], owners, live)
    rows = routed.shape[0]
    scaled = (gate_row * out_cot.astype(f32)).astype(bf16)
    gate_pre = jnp.dot(routed, weights[0, 0], preferred_element_type=f32)
    up_pre = jnp.dot(routed, weights[0, 1], preferred_element_type=f32)
    hidden_grad = jnp.dot(scaled, weights[0, 2], preferred_element_type=f32)
    small = jnp.concatenate(backward_parts(gate_pre, up_pre, hidden_grad), axis=1)
    sides = [routed.reshape(rows, 2 * chips, width), scaled.reshape(rows, 2 * chips, width)]
    slices = jnp.concatenate(sides, axis=2).transpose(1, 0, 2)
    return slices, small


def gram_plain(lefts, rights):
    grams = []
    for left, right in zip(lefts, rights, strict=True):
        each = jnp.einsum("rnd,rnf->rdf", left, right, preferred_element_type=f32)
        grams.append(jnp.einsum("rdf,sdf->rs", each, each, precision=HIGHEST))
    return jnp.stack(grams)


def final_plain(coefs, lefts, rights, momentum):
    combined = []
    for t in range(3):
        right = (coefs[t][:, None, None] * rights[t].astype(f32)).astype(bf16)
        left = lefts[t].reshape(-1, lefts[t].shape[2])
        combined.append(
            lax.dot_general(
                left, right.reshape(-1, right.shape[2]), contract_rows, preferred_element_type=f32
            )
        )
    return moment_decay * momentum + (1.0 - moment_decay) * jnp.stack(combined)[None]


def back_plain(small, weights, sizes):
    owners, live, ff = sizes[0], sizes[2], sizes[5]
    grad = lax.dot_general(small[:, :ff], weights[0, 0], contract_cols, preferred_element_type=f32)
    grad = grad + lax.dot_general(
        small[:, ff : 2 * ff], weights[0, 1], contract_cols, preferred_element_type=f32
    )
    return grad.astype(bf16).reshape(owners, live, -1)


def token_plain(route_pos, returned, cap):
    owners, live, depth = returned.shape
    place = route_pos[0] // cap * live + route_pos[0] % cap
    picks = jnp.sum(place[:, :, None] == jnp.arange(owners * live)[None, None, :], axis=1)
    returned = returned.reshape(owners * live, depth)
    return jnp.dot(picks.astype(bf16), returned, preferred_element_type=f32).astype(bf16)[None]


def all_swaps(blocks, axis, scale=1):
    return [swap(block, axis, k * scale) if k else block for k, block in enumerate(blocks)]


def core_swaps(blocks):
    return [block for mine in blocks for block in (mine, swap(mine, "rep", 1))]


def with_kernels(x_rows, row_cot, gate_vals, route_pos, weights, momentum, sizes):
    owners, cap, live, chips, width, ff = sizes
    pairs = pack_call(x_rows, row_cot, gate_vals, sizes)
    tall = all_swaps(pairs, "rep", 2)
    small = forward_call(pairs, weights, sizes)
    wide = all_swaps([small] * chips, "rep", 2)
    returned = all_swaps(back_call(small, weights, sizes), "exp")
    token_grad = token_call(route_pos, returned, cap)
    wide, tall = core_swaps(wide), core_swaps(tall)
    tall_gram, flip = tall_call(tall)
    gram = gram_call(wide, tall_gram, ff)
    mask = chips
    while mask > 2:
        gram = gram + swap(gram, "rep", mask)
        mask //= 2
    other = swap(gram, "rep", 2)
    return token_grad, final_call(gram, other, flip, wide, momentum, ff)


def without_kernels(x_rows, row_cot, gate_vals, route_pos, weights, momentum, sizes):
    owners, cap, live, chips, width, ff = sizes
    reps = 2 * chips
    slices, small = forward_plain(x_rows, row_cot, gate_vals, weights, sizes)
    tall = lax.all_to_all(slices, "rep", split_axis=0, concat_axis=0, tiled=True)
    wide = jnp.stack(core_swaps(all_swaps([small] * chips, "rep", 2)))
    returned = back_plain(small, weights, sizes)
    returned = lax.all_to_all(returned, "exp", split_axis=0, concat_axis=0, tiled=True)
    token_grad = token_plain(route_pos, returned, cap)
    order = jnp.arange(reps) ^ lax.axis_index("rep")
    tall = tall[order]
    lefts = [tall[:, :, :width], tall[:, :, :width], tall[:, :, width:]]
    rights = [wide[:, :, t * ff : (t + 1) * ff] for t in range(3)]
    gram = gram_plain(lefts, rights)[:, order][:, :, order]
    mask = chips
    while mask >= 1:
        gram = gram + swap(gram, "rep", mask)
        mask //= 2
    return token_grad, final_plain(adasum_weights(gram)[:, order], lefts, rights, momentum)


def on_device(x_rows, row_cot, gate_vals, route_pos, weights, momentum):
    reps = lax.axis_size("rep")
    owners = lax.axis_size("exp")
    cap = x_rows.shape[1] // owners
    live = min(cap, route_pos.shape[1])
    width = x_rows.shape[2] // reps
    ff = weights.shape[3]
    sizes = (owners, cap, live, reps // 2, width, ff)
    fits = width % 128 == 0 and ff % 128 == 0 and owners * live % 16 == 0 and reps == 8
    body = with_kernels if fits else without_kernels
    return body(x_rows, row_cot, gate_vals, route_pos, weights, momentum, sizes)


def solution(mesh):
    placed = (
        P("rep", "exp", None),
        P("rep", "exp", None),
        P("rep", "exp"),
        P("rep", "exp", None),
        P("exp", None, None, None),
        P("exp", None, "rep", None),
    )
    return jax.shard_map(
        on_device,
        mesh=mesh,
        in_specs=placed,
        out_specs=(P("rep", "exp", None), P("exp", None, "rep", None)),
        check_vma=False,
    )
```

```python
import functools

import jax
import jax.numpy as jnp
from jax import lax
from jax.experimental import pallas as pl
from jax.experimental.pallas import tpu as pltpu
from jax.sharding import PartitionSpec as P

tiny_eps = 1e-06
moment_decay = 0.9
HIGHEST = lax.Precision.HIGHEST
pack_flops = 10**11
bf16, f32 = jnp.bfloat16, jnp.float32
contract_rows = (((0,), (0,)), ((), ()))
contract_cols = (((1,), (1,)), ((), ()))


def swap(block, axis, mask):
    count = lax.axis_size(axis)
    return lax.ppermute(block, axis, [(i, i ^ mask) for i in range(count)])


def live_rows(block, owners, live):
    width = block.shape[-1]
    return block.reshape(owners, -1, width)[:, :live].reshape(owners * live, width)


def backward_parts(gate_pre, up_pre, hidden_grad):
    sigma_gate = jax.nn.sigmoid(gate_pre)
    activation = gate_pre * sigma_gate
    hidden = (activation * up_pre).astype(bf16)
    gate_grad = (hidden_grad * up_pre * sigma_gate * (1.0 + gate_pre * (1.0 - sigma_gate))).astype(
        bf16
    )
    up_grad = (hidden_grad * activation).astype(bf16)
    return gate_grad, up_grad, hidden


VMEM = pl.BlockSpec(memory_space=pltpu.VMEM)
HBM = pl.BlockSpec(memory_space=pltpu.HBM)


def in_hbm(array):
    return pltpu.with_memory_space_constraint(array, pltpu.HBM)


def kernel_params(mib):
    return pltpu.CompilerParams(vmem_limit_bytes=mib << 20)


def spread_rows(index, live, cap, owners):
    place = index
    for owner in range(1, owners):
        place = place + jnp.where(index >= owner * live, cap - live, 0)
    return place


def pack_kernel(sizes, x_hbm, cot_hbm, gate_hbm, *refs):
    owners, cap, live, chips, width, _ = sizes
    out_refs, (x_ref, cot_ref, gate_ref, sems, gate_sem) = refs[:chips], refs[chips:]
    slots, rows = owners * cap, owners * live
    chip = lax.axis_index("rep") >> 1
    gate_copy = pltpu.make_async_copy(gate_hbm, gate_ref, gate_sem)
    gate_copy.start()
    copies = []
    for k in range(chips):
        at = pl.ds(pl.multiple_of((chip ^ k) * 2 * width, 2 * width), 2 * width)
        for side, (source, target) in enumerate([(x_hbm, x_ref), (cot_hbm, cot_ref)]):
            copy = pltpu.make_async_copy(source.at[0, :, at], target.at[k], sems.at[k, side])
            copy.start()
            copies.append(copy)
    place = spread_rows(lax.broadcasted_iota(jnp.int32, (rows, slots), 0), live, cap, owners)
    slot = lax.broadcasted_iota(jnp.int32, (rows, slots), 1)
    select = jnp.where(place == slot, 1.0, 0.0).astype(bf16)
    line = lax.broadcasted_iota(jnp.int32, (slots, slots), 0)
    lane = lax.broadcasted_iota(jnp.int32, (slots, slots), 1)
    gate_copy.wait()
    gate = jnp.sum(jnp.where(line == lane, gate_ref[...], 0.0), axis=1, keepdims=True)
    for k in range(chips):
        copies[2 * k].wait()
        copies[2 * k + 1].wait()
        scaled = (gate * cot_ref[k].astype(f32)).astype(bf16)
        routed = jnp.dot(select, x_ref[k], preferred_element_type=f32).astype(bf16)
        scaled = jnp.dot(select, scaled, preferred_element_type=f32).astype(bf16)
        for core in range(2):
            out_refs[k][core, :, :width] = routed[:, core * width : (core + 1) * width]
            out_refs[k][core, :, width:] = scaled[:, core * width : (core + 1) * width]


def pack_call(x_rows, row_cot, gate_vals, sizes):
    owners, cap, live, chips, width, _ = sizes
    rows = owners * live
    return pl.pallas_call(
        functools.partial(pack_kernel, sizes),
        out_shape=[jax.ShapeDtypeStruct((2, rows, 2 * width), bf16)] * chips,
        in_specs=[HBM] * 3,
        out_specs=[VMEM] * chips,
        scratch_shapes=[
            pltpu.VMEM((chips, owners * cap, 2 * width), bf16),
            pltpu.VMEM((chips, owners * cap, 2 * width), bf16),
            pltpu.VMEM((1, owners * cap), f32),
            pltpu.SemaphoreType.DMA((chips, 2)),
            pltpu.SemaphoreType.DMA,
        ],
        compiler_params=kernel_params(6),
        cost_estimate=pl.CostEstimate(
            flops=pack_flops, bytes_accessed=8 * x_rows.size, transcendentals=0
        ),
        name="pack",
    )(in_hbm(x_rows), in_hbm(row_cot), in_hbm(gate_vals))


def forward_kernel(sizes, *refs):
    _, _, _, chips, width, ff = sizes
    pair_refs, w_ref, small_ref = refs[:chips], refs[chips], refs[chips + 1]
    chip = lax.axis_index("rep") >> 1
    sums = [None] * 3
    for k in range(chips):
        for core in range(2):
            at = pl.ds(pl.multiple_of(((chip ^ k) * 2 + core) * width, width), width)
            for t in range(3):
                left = pair_refs[k][core, :, width:] if t == 2 else pair_refs[k][core, :, :width]
                part = jnp.dot(left, w_ref[0, t, at, :], preferred_element_type=f32)
                sums[t] = part if sums[t] is None else sums[t] + part
    for t, part in enumerate(backward_parts(*sums)):
        small_ref[:, t * ff : (t + 1) * ff] = part


def forward_call(pairs, weights, sizes):
    owners, _, live, chips, _, ff = sizes
    rows = owners * live
    return pl.pallas_call(
        functools.partial(forward_kernel, sizes),
        out_shape=jax.ShapeDtypeStruct((rows, 3 * ff), bf16),
        in_specs=[VMEM] * (chips + 1),
        out_specs=VMEM,
        compiler_params=kernel_params(7),
        cost_estimate=pl.CostEstimate(
            flops=2 * rows * weights.size,
            bytes_accessed=2 * weights.size,
            transcendentals=rows * ff,
        ),
        name="forward",
    )(*pairs, weights)


def back_kernel(sizes, small_ref, w_ref, *out_refs):
    owners, cap, live, chips, width, ff = sizes
    slots, rows = owners * cap, owners * live
    me = lax.axis_index("exp")
    slot = lax.broadcasted_iota(jnp.int32, (slots, rows), 0)
    row = lax.broadcasted_iota(jnp.int32, (slots, rows), 1)
    place = jnp.full((slots, rows), -1, jnp.int32)
    for k in range(owners):
        inside = (slot >= k * cap) & (slot < k * cap + live)
        place = jnp.where(inside, slot - k * cap + (me ^ k) * live, place)
    select = jnp.where(place == row, 1.0, 0.0).astype(bf16)
    spread = jnp.dot(select, small_ref[:, : 2 * ff], preferred_element_type=f32).astype(bf16)
    chunk = 2 * width
    for c in range(chips):
        at = slice(c * chunk, (c + 1) * chunk)
        grad = lax.dot_general(
            spread[:, :ff], w_ref[0, 0, at, :], contract_cols, preferred_element_type=f32
        ) + lax.dot_general(
            spread[:, ff:], w_ref[0, 1, at, :], contract_cols, preferred_element_type=f32
        )
        grad = grad.astype(bf16)
        for k in range(owners):
            out_refs[k][:, at] = grad[k * cap : k * cap + live]


def back_call(small, weights, sizes):
    owners, _, live, _, _, ff = sizes
    rows, depth = owners * live, weights.shape[2]
    return pl.pallas_call(
        functools.partial(back_kernel, sizes),
        out_shape=[jax.ShapeDtypeStruct((live, depth), bf16)] * owners,
        in_specs=[VMEM] * 2,
        out_specs=[VMEM] * owners,
        compiler_params=kernel_params(7),
        cost_estimate=pl.CostEstimate(
            flops=4 * rows * depth * ff,
            bytes_accessed=weights.size * 4 // 3,
            transcendentals=0,
        ),
        name="back",
    )(small, weights)


def token_kernel(cap, route_ref, *refs):
    row_refs, out_ref, held = refs[:-2], refs[-2], refs[-1]
    owners, live = len(row_refs), row_refs[0].shape[0]
    me = lax.axis_index("exp")
    held[...] = jnp.zeros_like(held)
    for k in range(owners):
        held[k * cap : k * cap + live] = row_refs[k][...]
    picks, tokens = route_ref.shape[1:]
    line = lax.broadcasted_iota(jnp.int32, (owners * cap, tokens), 0)
    place = line
    for k in range(owners):
        inside = (line >= k * cap) & (line < (k + 1) * cap)
        place = jnp.where(inside, line + ((me ^ k) - k) * cap, place)
    choice = jnp.zeros((owners * cap, tokens), f32)
    for pick in range(picks):
        choice = choice + jnp.where(route_ref[0, pick : pick + 1, :] == place, 1.0, 0.0)
    sums = lax.dot_general(
        choice.astype(bf16), held[...], contract_rows, preferred_element_type=f32
    )
    out_ref[0] = sums.astype(bf16)


def token_call(route_pos, returned, cap):
    owners, (live, depth) = len(returned), returned[0].shape
    return pl.pallas_call(
        functools.partial(token_kernel, cap),
        out_shape=jax.ShapeDtypeStruct((1, route_pos.shape[1], depth), bf16),
        in_specs=[VMEM] * (owners + 1),
        out_specs=VMEM,
        scratch_shapes=[pltpu.VMEM((owners * cap, depth), bf16)],
        compiler_params=kernel_params(6),
        cost_estimate=pl.CostEstimate(
            flops=2 * route_pos.shape[1] * owners * cap * depth,
            bytes_accessed=owners * live * depth * 4,
            transcendentals=0,
        ),
        name="token",
    )(route_pos.swapaxes(1, 2), *returned)


def tall_kernel(reps, *refs):
    tall_refs, gram_ref, flip_ref = refs[:reps], refs[reps], refs[reps + 1]
    width = tall_refs[0].shape[2] // 2
    core = lax.axis_index("rep") & 1
    for side in range(2):
        at = slice(side * width, (side + 1) * width)
        both = jnp.concatenate(
            [jnp.concatenate([ref[0, :, at], ref[1, :, at]], axis=1) for ref in tall_refs], axis=0
        )
        gram_ref[side] = lax.dot_general(both, both, contract_cols, preferred_element_type=f32)
        own = jnp.concatenate([ref[core, :, at] for ref in tall_refs], axis=0)
        flip_ref[side] = own.T


def tall_call(tall):
    reps, (cores, rows, width) = len(tall), tall[0].shape
    width //= 2
    flat = reps * rows
    return pl.pallas_call(
        functools.partial(tall_kernel, reps),
        out_shape=[
            jax.ShapeDtypeStruct((2, flat, flat), f32),
            jax.ShapeDtypeStruct((2, width, flat), bf16),
        ],
        in_specs=[VMEM] * reps,
        out_specs=[VMEM] * 2,
        compiler_params=kernel_params(6),
        cost_estimate=pl.CostEstimate(
            flops=8 * flat * flat * width,
            bytes_accessed=8 * flat * flat + 12 * flat * width,
            transcendentals=0,
        ),
        name="tall",
    )(*tall)


def gram_kernel(reps, ff, *refs):
    wide_refs, tall_ref, out_ref = refs[:reps], refs[reps], refs[reps + 1]
    rows = wide_refs[0].shape[0]
    flat = reps * rows
    me = lax.axis_index("rep")
    spot = lax.broadcasted_iota(jnp.int32, (flat, 128), 0)
    lane = lax.broadcasted_iota(jnp.int32, (flat, 128), 1)
    group = jnp.zeros_like(spot)
    for k in range(1, reps):
        group = group + jnp.where(spot >= k * rows, 1, 0)
    gather = jnp.where((group ^ me) == (lane & (reps - 1)), 1.0, 0.0)
    sums = []
    for t in range(3):
        block = jnp.concatenate([ref[:, t * ff : (t + 1) * ff] for ref in wide_refs], axis=0)
        both = lax.dot_general(block, block, contract_cols, preferred_element_type=f32)
        both = both * tall_ref[t // 2]
        sums.append(jnp.sum(both.reshape(reps, rows // 8, 8, flat), axis=1).reshape(reps * 8, flat))
    sums = jnp.dot(
        jnp.concatenate(sums, axis=0), gather, precision=HIGHEST, preferred_element_type=f32
    )
    sums = jnp.sum(sums.reshape(3 * reps, 8, 128), axis=1)
    for t in range(3):
        for k in range(reps):
            out_ref[pl.ds(t * reps + (me ^ k), 1), :] = sums[t * reps + k : t * reps + k + 1]


def gram_call(wide, tall_gram, ff):
    reps, rows = len(wide), wide[0].shape[0]
    flat = reps * rows
    return pl.pallas_call(
        functools.partial(gram_kernel, reps, ff),
        out_shape=jax.ShapeDtypeStruct((3 * reps, 128), f32),
        in_specs=[VMEM] * (reps + 1),
        out_specs=VMEM,
        compiler_params=kernel_params(6),
        cost_estimate=pl.CostEstimate(
            flops=6 * flat * flat * ff,
            bytes_accessed=8 * flat * flat + 6 * flat * ff,
            transcendentals=0,
        ),
        name="gram",
    )(*wide, tall_gram)


def final_kernel(reps, ff, gram_ref, other_ref, flip_ref, *refs):
    wide_refs, moment_ref, out_ref, coef_ref = refs[:reps], refs[reps], refs[reps + 1], refs[reps + 2]
    me = lax.axis_index("rep")
    line = lax.broadcasted_iota(jnp.int32, (reps, 128), 0)
    lane = lax.broadcasted_iota(jnp.int32, (reps, 128), 1)
    near = lane & (reps - 1)
    for t in range(3):
        part = slice(t * reps, (t + 1) * reps)
        gram = gram_ref[part, :] + other_ref[part, :]
        coefs = jnp.ones((reps, 128), f32)
        half = reps // 2
        while half >= 1:

            def factor(axis, spot):
                square = jnp.where(spot == line, gram, 0.0)
                square = jnp.maximum(jnp.sum(square, axis=axis, keepdims=True), 0.0)
                square = jnp.broadcast_to(square, (reps, 128))
                inner = jnp.where(spot == line ^ half, gram, 0.0)
                inner = jnp.sum(inner, axis=axis, keepdims=True)
                bound = jnp.sqrt(square * pltpu.roll(square, half, 1 - axis))
                inner = jnp.clip(inner, -bound, bound)
                return 1.0 - inner / (2.0 * (square + tiny_eps))

            by_line, by_lane = factor(1, lane), factor(0, near)
            coefs = coefs * by_line
            gram = gram * by_line * by_lane
            gram = gram + pltpu.roll(gram, half, 0)
            gram = gram + pltpu.roll(gram, half, 1)
            half //= 2
        coef_ref[part, :] = jnp.concatenate([coefs] * (ff // 128), axis=1)
    for t in range(3):
        scaled = []
        for k in range(reps):
            coef = coef_ref[pl.ds(t * reps + (me ^ k), 1), :]
            scaled.append((coef * wide_refs[k][:, t * ff : (t + 1) * ff].astype(f32)).astype(bf16))
        combined = jnp.dot(
            flip_ref[t // 2], jnp.concatenate(scaled, axis=0), preferred_element_type=f32
        )
        out_ref[0, t] = moment_decay * moment_ref[0, t] + (1.0 - moment_decay) * combined


def final_call(gram, other, flip, wide, momentum, ff):
    reps, rows = len(wide), wide[0].shape[0]
    return pl.pallas_call(
        functools.partial(final_kernel, reps, ff),
        out_shape=jax.ShapeDtypeStruct(momentum.shape, f32),
        in_specs=[VMEM] * (reps + 4),
        out_specs=VMEM,
        scratch_shapes=[pltpu.VMEM((3 * reps, ff), f32)],
        compiler_params=kernel_params(6),
        cost_estimate=pl.CostEstimate(
            flops=2 * reps * rows * momentum.size,
            bytes_accessed=8 * momentum.size + 6 * reps * rows * ff,
            transcendentals=0,
        ),
        name="final",
    )(gram, other, flip, *wide, momentum)


def adasum_weights(gram):
    count = gram.shape[-1]
    index = jnp.arange(count)
    weights = jnp.ones(gram.shape[:2], f32)
    half = count // 2
    while half >= 1:
        partner = index ^ half
        square = jnp.maximum(jnp.sum(jnp.where(index[:, None] == index[None, :], gram, 0.0), 2), 0.0)
        inner = jnp.sum(jnp.where(partner[:, None] == index[None, :], gram, 0.0), 2)
        bound = jnp.sqrt(square * square[:, partner])
        inner = jnp.clip(inner, -bound, bound)
        coef = 1.0 - inner / (2.0 * (square + tiny_eps))
        weights = weights * coef
        gram = gram * coef[:, :, None] * coef[:, None, :]
        gram = gram + gram[:, partner]
        gram = gram + gram[:, :, partner]
        half //= 2
    return weights


def forward_plain(x_rows, row_cot, gate_vals, weights, sizes):
    owners, _, live, chips, width, _ = sizes
    routed = live_rows(x_rows[0], owners, live)
    out_cot = live_rows(row_cot[0], owners, live)
    gate_row = live_rows(gate_vals[0][:, None], owners, live)
    rows = routed.shape[0]
    scaled = (gate_row * out_cot.astype(f32)).astype(bf16)
    gate_pre = jnp.dot(routed, weights[0, 0], preferred_element_type=f32)
    up_pre = jnp.dot(routed, weights[0, 1], preferred_element_type=f32)
    hidden_grad = jnp.dot(scaled, weights[0, 2], preferred_element_type=f32)
    small = jnp.concatenate(backward_parts(gate_pre, up_pre, hidden_grad), axis=1)
    sides = [routed.reshape(rows, 2 * chips, width), scaled.reshape(rows, 2 * chips, width)]
    slices = jnp.concatenate(sides, axis=2).transpose(1, 0, 2)
    return slices, small


def gram_plain(lefts, rights):
    grams = []
    for left, right in zip(lefts, rights, strict=True):
        each = jnp.einsum("rnd,rnf->rdf", left, right, preferred_element_type=f32)
        grams.append(jnp.einsum("rdf,sdf->rs", each, each, precision=HIGHEST))
    return jnp.stack(grams)


def final_plain(coefs, lefts, rights, momentum):
    combined = []
    for t in range(3):
        right = (coefs[t][:, None, None] * rights[t].astype(f32)).astype(bf16)
        left = lefts[t].reshape(-1, lefts[t].shape[2])
        combined.append(
            lax.dot_general(
                left, right.reshape(-1, right.shape[2]), contract_rows, preferred_element_type=f32
            )
        )
    return moment_decay * momentum + (1.0 - moment_decay) * jnp.stack(combined)[None]


def back_plain(small, weights, sizes):
    owners, live, ff = sizes[0], sizes[2], sizes[5]
    grad = lax.dot_general(small[:, :ff], weights[0, 0], contract_cols, preferred_element_type=f32)
    grad = grad + lax.dot_general(
        small[:, ff : 2 * ff], weights[0, 1], contract_cols, preferred_element_type=f32
    )
    return grad.astype(bf16).reshape(owners, live, -1)


def token_plain(route_pos, returned, cap):
    owners, live, depth = returned.shape
    place = route_pos[0] // cap * live + route_pos[0] % cap
    picks = jnp.sum(place[:, :, None] == jnp.arange(owners * live)[None, None, :], axis=1)
    returned = returned.reshape(owners * live, depth)
    return jnp.dot(picks.astype(bf16), returned, preferred_element_type=f32).astype(bf16)[None]


def all_swaps(blocks, axis, scale):
    got = []
    for k, block in enumerate(blocks):
        got.append(swap(block, axis, k * scale) if k else block)
    return got


def core_swaps(blocks):
    got = []
    for mine in blocks:
        got += [mine, swap(mine, "rep", 1)]
    return got


def with_kernels(x_rows, row_cot, gate_vals, route_pos, weights, momentum, sizes):
    _, cap, _, chips, _, ff = sizes
    pairs = pack_call(x_rows, row_cot, gate_vals, sizes)
    tall = all_swaps(pairs, "rep", 2)
    small = forward_call(pairs, weights, sizes)
    wide = all_swaps([small] * chips, "rep", 2)
    returned = all_swaps(back_call(small, weights, sizes), "exp", 1)
    token_grad = token_call(route_pos, returned, cap)
    tall, wide = core_swaps(tall), core_swaps(wide)
    tall_gram, flip = tall_call(tall)
    gram = gram_call(wide, tall_gram, ff)
    mask = chips
    while mask > 2:
        gram = gram + swap(gram, "rep", mask)
        mask //= 2
    other = swap(gram, "rep", 2)
    return token_grad, final_call(gram, other, flip, wide, momentum, ff)


def without_kernels(x_rows, row_cot, gate_vals, route_pos, weights, momentum, sizes):
    _, cap, _, chips, width, ff = sizes
    reps = 2 * chips
    slices, small = forward_plain(x_rows, row_cot, gate_vals, weights, sizes)
    tall = lax.all_to_all(slices, "rep", split_axis=0, concat_axis=0, tiled=True)
    wide = jnp.stack(core_swaps(all_swaps([small] * chips, "rep", 2)))
    returned = back_plain(small, weights, sizes)
    returned = lax.all_to_all(returned, "exp", split_axis=0, concat_axis=0, tiled=True)
    token_grad = token_plain(route_pos, returned, cap)
    order = jnp.arange(reps) ^ lax.axis_index("rep")
    tall = tall[order]
    lefts = [tall[:, :, :width], tall[:, :, :width], tall[:, :, width:]]
    rights = [wide[:, :, t * ff : (t + 1) * ff] for t in range(3)]
    gram = gram_plain(lefts, rights)[:, order][:, :, order]
    mask = chips
    while mask >= 1:
        gram = gram + swap(gram, "rep", mask)
        mask //= 2
    return token_grad, final_plain(adasum_weights(gram)[:, order], lefts, rights, momentum)


def on_device(x_rows, row_cot, gate_vals, route_pos, weights, momentum):
    reps = lax.axis_size("rep")
    owners = lax.axis_size("exp")
    cap = x_rows.shape[1] // owners
    live = min(cap, route_pos.shape[1])
    width = x_rows.shape[2] // reps
    ff = weights.shape[3]
    sizes = (owners, cap, live, reps // 2, width, ff)
    body = with_kernels if kernels_fit(reps, owners, live, width, ff) else without_kernels
    return body(x_rows, row_cot, gate_vals, route_pos, weights, momentum, sizes)


def kernels_fit(reps, owners, live, width, ff):
    return width % 128 == 0 and ff % 128 == 0 and owners * live % 16 == 0 and reps == 8


def solution(mesh):
    placed = (
        P("rep", "exp", None),
        P("rep", "exp", None),
        P("rep", "exp"),
        P("rep", "exp", None),
        P("exp", None, None, None),
        P("exp", None, "rep", None),
    )
    return jax.shard_map(
        on_device,
        mesh=mesh,
        in_specs=placed,
        out_specs=(P("rep", "exp", None), P("exp", None, "rep", None)),
        check_vma=False,
    )
```

```python
import functools

import jax
import jax.numpy as jnp
from jax import lax
from jax.experimental import pallas as pl
from jax.experimental.pallas import tpu as pltpu
from jax.sharding import PartitionSpec as P

tiny_eps = 1e-06
moment_decay = 0.9
HIGHEST = lax.Precision.HIGHEST
pack_flops = 10**11
bf16, f32 = jnp.bfloat16, jnp.float32
contract_rows = (((0,), (0,)), ((), ()))
contract_cols = (((1,), (1,)), ((), ()))


def swap(block, axis, mask):
    count = lax.axis_size(axis)
    return lax.ppermute(block, axis, [(i, i ^ mask) for i in range(count)])


def turn_step(core, turn):
    return turn if turn in (0, 3) else turn ^ 3 ^ (3 * core)


def turn_swap(block, turn):
    count = lax.axis_size("rep")
    route = [(i, i ^ (2 * turn_step(i & 1, turn))) for i in range(count)]
    return lax.ppermute(block, "rep", route)


block_order = (0, 1, 2, 4, 6, 3, 5, 7)
late_blocks = 3


def replica_of(me, place):
    core, block = me & 1, block_order[place]
    if block & 1:
        core, me = 1 - core, me ^ 1
    return me ^ (2 * turn_step(core, block >> 1))


def live_rows(block, owners, live):
    width = block.shape[-1]
    return block.reshape(owners, -1, width)[:, :live].reshape(owners * live, width)


def backward_parts(gate_pre, up_pre, hidden_grad):
    sigma_gate = jax.nn.sigmoid(gate_pre)
    activation = gate_pre * sigma_gate
    hidden = (activation * up_pre).astype(bf16)
    gate_grad = (hidden_grad * up_pre * sigma_gate * (1.0 + gate_pre * (1.0 - sigma_gate))).astype(
        bf16
    )
    up_grad = (hidden_grad * activation).astype(bf16)
    return gate_grad, up_grad, hidden


VMEM = pl.BlockSpec(memory_space=pltpu.VMEM)
HBM = pl.BlockSpec(memory_space=pltpu.HBM)


def in_hbm(array):
    return pltpu.with_memory_space_constraint(array, pltpu.HBM)


def kernel_params(mib):
    return pltpu.CompilerParams(vmem_limit_bytes=mib << 20)


def spread_rows(index, live, cap, owners):
    place = index
    for owner in range(1, owners):
        place = place + jnp.where(index >= owner * live, cap - live, 0)
    return place


def pack_kernel(sizes, x_hbm, cot_hbm, gate_hbm, *refs):
    owners, cap, live, chips, width, _ = sizes
    out_refs, (x_ref, cot_ref, gate_ref, sems, gate_sem) = refs[:chips], refs[chips:]
    slots, rows = owners * cap, owners * live
    me = lax.axis_index("rep")
    gate_copy = pltpu.make_async_copy(gate_hbm, gate_ref, gate_sem)
    gate_copy.start()
    copies = []
    for k in range(chips):
        chip = (me >> 1) ^ turn_step(me & 1, k)
        at = pl.ds(pl.multiple_of(chip * 2 * width, 2 * width), 2 * width)
        for side, (source, target) in enumerate([(x_hbm, x_ref), (cot_hbm, cot_ref)]):
            copy = pltpu.make_async_copy(source.at[0, :, at], target.at[k], sems.at[k, side])
            copy.start()
            copies.append(copy)
    place = spread_rows(lax.broadcasted_iota(jnp.int32, (rows, slots), 0), live, cap, owners)
    slot = lax.broadcasted_iota(jnp.int32, (rows, slots), 1)
    select = jnp.where(place == slot, 1.0, 0.0).astype(bf16)
    line = lax.broadcasted_iota(jnp.int32, (slots, slots), 0)
    lane = lax.broadcasted_iota(jnp.int32, (slots, slots), 1)
    gate_copy.wait()
    gate = jnp.sum(jnp.where(line == lane, gate_ref[...], 0.0), axis=1, keepdims=True)
    for k in range(chips):
        copies[2 * k].wait()
        copies[2 * k + 1].wait()
        scaled = (gate * cot_ref[k].astype(f32)).astype(bf16)
        routed = jnp.dot(select, x_ref[k], preferred_element_type=f32).astype(bf16)
        scaled = jnp.dot(select, scaled, preferred_element_type=f32).astype(bf16)
        for core in range(2):
            out_refs[k][core, :, :width] = routed[:, core * width : (core + 1) * width]
            out_refs[k][core, :, width:] = scaled[:, core * width : (core + 1) * width]


def pack_call(x_rows, row_cot, gate_vals, sizes):
    owners, cap, live, chips, width, _ = sizes
    rows = owners * live
    return pl.pallas_call(
        functools.partial(pack_kernel, sizes),
        out_shape=[jax.ShapeDtypeStruct((2, rows, 2 * width), bf16)] * chips,
        in_specs=[HBM] * 3,
        out_specs=[VMEM] * chips,
        scratch_shapes=[
            pltpu.VMEM((chips, owners * cap, 2 * width), bf16),
            pltpu.VMEM((chips, owners * cap, 2 * width), bf16),
            pltpu.VMEM((1, owners * cap), f32),
            pltpu.SemaphoreType.DMA((chips, 2)),
            pltpu.SemaphoreType.DMA,
        ],
        compiler_params=kernel_params(6),
        cost_estimate=pl.CostEstimate(
            flops=pack_flops, bytes_accessed=8 * x_rows.size, transcendentals=0
        ),
        name="pack",
    )(in_hbm(x_rows), in_hbm(row_cot), in_hbm(gate_vals))


def forward_kernel(sizes, *refs):
    _, _, _, chips, width, ff = sizes
    pair_refs, w_ref, small_ref = refs[:chips], refs[chips], refs[chips + 1]
    me = lax.axis_index("rep")
    sums = [None] * 3
    for k in range(chips):
        chip = (me >> 1) ^ turn_step(me & 1, k)
        for core in range(2):
            at = pl.ds(pl.multiple_of((chip * 2 + core) * width, width), width)
            for t in range(3):
                left = pair_refs[k][core, :, width:] if t == 2 else pair_refs[k][core, :, :width]
                part = jnp.dot(left, w_ref[0, t, at, :], preferred_element_type=f32)
                sums[t] = part if sums[t] is None else sums[t] + part
    for t, part in enumerate(backward_parts(*sums)):
        small_ref[:, t * ff : (t + 1) * ff] = part


def forward_call(pairs, weights, sizes):
    owners, _, live, chips, _, ff = sizes
    rows = owners * live
    return pl.pallas_call(
        functools.partial(forward_kernel, sizes),
        out_shape=jax.ShapeDtypeStruct((rows, 3 * ff), bf16),
        in_specs=[VMEM] * (chips + 1),
        out_specs=VMEM,
        compiler_params=kernel_params(7),
        cost_estimate=pl.CostEstimate(
            flops=2 * rows * weights.size,
            bytes_accessed=2 * weights.size,
            transcendentals=rows * ff,
        ),
        name="forward",
    )(*pairs, weights)


def back_kernel(sizes, small_ref, w_ref, *out_refs):
    owners, cap, live, chips, width, ff = sizes
    slots, rows = owners * cap, owners * live
    me = lax.axis_index("exp")
    slot = lax.broadcasted_iota(jnp.int32, (slots, rows), 0)
    row = lax.broadcasted_iota(jnp.int32, (slots, rows), 1)
    place = jnp.full((slots, rows), -1, jnp.int32)
    for k in range(owners):
        inside = (slot >= k * cap) & (slot < k * cap + live)
        place = jnp.where(inside, slot - k * cap + (me ^ k) * live, place)
    select = jnp.where(place == row, 1.0, 0.0).astype(bf16)
    spread = jnp.dot(select, small_ref[:, : 2 * ff], preferred_element_type=f32).astype(bf16)
    chunk = 2 * width
    for c in range(chips):
        at = slice(c * chunk, (c + 1) * chunk)
        grad = lax.dot_general(
            spread[:, :ff], w_ref[0, 0, at, :], contract_cols, preferred_element_type=f32
        ) + lax.dot_general(
            spread[:, ff:], w_ref[0, 1, at, :], contract_cols, preferred_element_type=f32
        )
        grad = grad.astype(bf16)
        for k in range(owners):
            out_refs[k][:, at] = grad[k * cap : k * cap + live]


def back_call(small, weights, sizes):
    owners, _, live, _, _, ff = sizes
    rows, depth = owners * live, weights.shape[2]
    return pl.pallas_call(
        functools.partial(back_kernel, sizes),
        out_shape=[jax.ShapeDtypeStruct((live, depth), bf16)] * owners,
        in_specs=[VMEM] * 2,
        out_specs=[VMEM] * owners,
        compiler_params=kernel_params(7),
        cost_estimate=pl.CostEstimate(
            flops=4 * rows * depth * ff,
            bytes_accessed=weights.size * 4 // 3,
            transcendentals=0,
        ),
        name="back",
    )(small, weights)


def token_kernel(cap, route_ref, *refs):
    row_refs, out_ref, held = refs[:-2], refs[-2], refs[-1]
    owners, live = len(row_refs), row_refs[0].shape[0]
    me = lax.axis_index("exp")
    held[...] = jnp.zeros_like(held)
    for k in range(owners):
        held[k * cap : k * cap + live] = row_refs[k][...]
    picks, tokens = route_ref.shape[1:]
    line = lax.broadcasted_iota(jnp.int32, (owners * cap, tokens), 0)
    place = line
    for k in range(owners):
        inside = (line >= k * cap) & (line < (k + 1) * cap)
        place = jnp.where(inside, line + ((me ^ k) - k) * cap, place)
    choice = jnp.zeros((owners * cap, tokens), f32)
    for pick in range(picks):
        choice = choice + jnp.where(route_ref[0, pick : pick + 1, :] == place, 1.0, 0.0)
    sums = lax.dot_general(
        choice.astype(bf16), held[...], contract_rows, preferred_element_type=f32
    )
    out_ref[0] = sums.astype(bf16)


def token_call(route_pos, returned, cap):
    owners, (live, depth) = len(returned), returned[0].shape
    return pl.pallas_call(
        functools.partial(token_kernel, cap),
        out_shape=jax.ShapeDtypeStruct((1, route_pos.shape[1], depth), bf16),
        in_specs=[VMEM] * (owners + 1),
        out_specs=VMEM,
        scratch_shapes=[pltpu.VMEM((owners * cap, depth), bf16)],
        compiler_params=kernel_params(6),
        cost_estimate=pl.CostEstimate(
            flops=2 * route_pos.shape[1] * owners * cap * depth,
            bytes_accessed=owners * live * depth * 4,
            transcendentals=0,
        ),
        name="token",
    )(route_pos.swapaxes(1, 2), *returned)


def tall_kernel(reps, *refs):
    tall_refs, gram_ref, flip_ref = refs[:reps], refs[reps], refs[reps + 1]
    width = tall_refs[0].shape[2] // 2
    core = lax.axis_index("rep") & 1
    for side in range(2):
        at = slice(side * width, (side + 1) * width)
        both = jnp.concatenate(
            [jnp.concatenate([ref[0, :, at], ref[1, :, at]], axis=1) for ref in tall_refs], axis=0
        )
        gram_ref[side] = lax.dot_general(both, both, contract_cols, preferred_element_type=f32)
        own = jnp.concatenate([ref[core, :, at] for ref in tall_refs], axis=0)
        flip_ref[side] = own.T


def tall_call(tall):
    reps, (cores, rows, width) = len(tall), tall[0].shape
    width //= 2
    flat = reps * rows
    return pl.pallas_call(
        functools.partial(tall_kernel, reps),
        out_shape=[
            jax.ShapeDtypeStruct((2, flat, flat), f32),
            jax.ShapeDtypeStruct((2, width, flat), bf16),
        ],
        in_specs=[VMEM] * reps,
        out_specs=[VMEM] * 2,
        compiler_params=kernel_params(6),
        cost_estimate=pl.CostEstimate(
            flops=8 * flat * flat * width,
            bytes_accessed=8 * flat * flat + 12 * flat * width,
            transcendentals=0,
        ),
        name="tall",
    )(*tall)


def pair_sums(wide_refs, tall_ref, ff, me, start):
    reps, rows = len(wide_refs), wide_refs[0].shape[0]
    flat = reps * rows
    spot = lax.broadcasted_iota(jnp.int32, (flat, 128), 0)
    lane = lax.broadcasted_iota(jnp.int32, (flat, 128), 1)
    group = jnp.full_like(spot, me)
    for k in range(1, reps):
        group = jnp.where(spot >= k * rows, replica_of(me, k), group)
    gather = jnp.where(group == (lane & 7), 1.0, 0.0)
    sums = []
    for t in range(3):
        block = jnp.concatenate([ref[:, t * ff : (t + 1) * ff] for ref in wide_refs], axis=0)
        both = lax.dot_general(
            block[start * rows :], block, contract_cols, preferred_element_type=f32
        )
        both = both * tall_ref[t // 2, start * rows : flat, :flat]
        both = both.reshape(reps - start, rows // 8, 8, flat)
        sums.append(jnp.sum(both, axis=1).reshape((reps - start) * 8, flat))
    sums = jnp.dot(
        jnp.concatenate(sums, axis=0), gather, precision=HIGHEST, preferred_element_type=f32
    )
    return jnp.sum(sums.reshape(3 * (reps - start), 8, 128), axis=1)


def first_kernel(reps, ff, *refs):
    wide_refs, tall_ref, out_ref = refs[:-2], refs[-2], refs[-1]
    me, count = lax.axis_index("rep"), len(wide_refs)
    sums = pair_sums(wide_refs, tall_ref, ff, me, 0)
    out_ref[...] = jnp.zeros_like(out_ref)
    for t in range(3):
        for k in range(count):
            at = pl.ds(t * reps + replica_of(me, k), 1)
            out_ref[at, :] = sums[t * count + k : t * count + k + 1]


def last_kernel(reps, ff, *refs):
    wide_refs, tall_ref, first_ref, out_ref = refs[:reps], refs[reps], refs[reps + 1], refs[reps + 2]
    me = lax.axis_index("rep")
    sums = pair_sums(wide_refs, tall_ref, ff, me, reps - late_blocks)
    line = lax.broadcasted_iota(jnp.int32, (reps, 128), 0)
    lane = lax.broadcasted_iota(jnp.int32, (reps, 128), 1)
    near = lane & (reps - 1)
    owns = [replica_of(me, k) for k in range(reps - late_blocks, reps)]
    old = line >= 0
    for own in owns:
        old = old & (line != own)
    for t in range(3):
        gram = first_ref[t * reps : (t + 1) * reps, :]
        for j, own in enumerate(owns):
            row = jnp.broadcast_to(sums[late_blocks * t + j : late_blocks * t + j + 1], (reps, 128))
            column = jnp.sum(jnp.where(line == lane, row, 0.0), axis=1, keepdims=True)
            gram = gram + jnp.where(line == own, row, 0.0)
            gram = gram + jnp.where(old & (near == own), column, 0.0)
        out_ref[t * reps : (t + 1) * reps, :] = gram


def gram_calls(wide, tall_gram, ff):
    reps, rows = len(wide), wide[0].shape[0]
    flat = reps * rows
    shape = jax.ShapeDtypeStruct((3 * reps, 128), f32)
    first = pl.pallas_call(
        functools.partial(first_kernel, reps, ff),
        out_shape=shape,
        in_specs=[VMEM] * (reps - late_blocks + 1),
        out_specs=VMEM,
        compiler_params=kernel_params(6),
        cost_estimate=pl.CostEstimate(
            flops=3 * flat * flat * ff,
            bytes_accessed=4 * flat * flat + 4 * flat * ff,
            transcendentals=0,
        ),
        name="first",
    )(*wide[:-late_blocks], tall_gram)
    return pl.pallas_call(
        functools.partial(last_kernel, reps, ff),
        out_shape=shape,
        in_specs=[VMEM] * (reps + 2),
        out_specs=VMEM,
        compiler_params=kernel_params(6),
        cost_estimate=pl.CostEstimate(
            flops=3 * flat * flat * ff // 2,
            bytes_accessed=2 * flat * flat + 6 * flat * ff,
            transcendentals=0,
        ),
        name="last",
    )(*wide, tall_gram, first)


def final_kernel(reps, ff, *refs):
    gram_refs, flip_ref, refs = refs[:2], refs[2], refs[3:]
    wide_refs, (moment_ref, out_hbm, coef_ref, out_ref, sems) = refs[:reps], refs[reps:]
    copies = []
    me = lax.axis_index("rep")
    line = lax.broadcasted_iota(jnp.int32, (reps, 128), 0)
    lane = lax.broadcasted_iota(jnp.int32, (reps, 128), 1)
    near = lane & (reps - 1)
    for t in range(3):
        part = slice(t * reps, (t + 1) * reps)
        gram = gram_refs[0][part, :] + gram_refs[1][part, :]
        coefs = jnp.ones((reps, 128), f32)
        half = reps // 2
        while half >= 1:

            def factor(axis, spot):
                square = jnp.where(spot == line, gram, 0.0)
                square = jnp.maximum(jnp.sum(square, axis=axis, keepdims=True), 0.0)
                square = jnp.broadcast_to(square, (reps, 128))
                inner = jnp.where(spot == line ^ half, gram, 0.0)
                inner = jnp.sum(inner, axis=axis, keepdims=True)
                bound = jnp.sqrt(square * pltpu.roll(square, half, 1 - axis))
                inner = jnp.clip(inner, -bound, bound)
                return 1.0 - inner / (2.0 * (square + tiny_eps))

            by_line, by_lane = factor(1, lane), factor(0, near)
            coefs = coefs * by_line
            gram = gram * by_line * by_lane
            gram = gram + pltpu.roll(gram, half, 0)
            gram = gram + pltpu.roll(gram, half, 1)
            half //= 2
        coef_ref[part, :] = jnp.concatenate([coefs] * (ff // 128), axis=1)
    for t in range(3):
        scaled = []
        for k in range(reps):
            coef = coef_ref[pl.ds(t * reps + replica_of(me, k), 1), :]
            scaled.append((coef * wide_refs[k][:, t * ff : (t + 1) * ff].astype(f32)).astype(bf16))
        combined = jnp.dot(
            flip_ref[t // 2], jnp.concatenate(scaled, axis=0), preferred_element_type=f32
        )
        out_ref[0, t] = moment_decay * moment_ref[0, t] + (1.0 - moment_decay) * combined
        copies.append(pltpu.make_async_copy(out_ref.at[0, t], out_hbm.at[0, t], sems.at[t]))
        copies[t].start()
    for copy in copies:
        copy.wait()


def final_call(grams, flip, wide, momentum, ff):
    reps, rows = len(wide), wide[0].shape[0]
    return pl.pallas_call(
        functools.partial(final_kernel, reps, ff),
        out_shape=jax.ShapeDtypeStruct(momentum.shape, f32),
        in_specs=[VMEM] * (len(grams) + reps + 2),
        out_specs=HBM,
        scratch_shapes=[
            pltpu.VMEM((3 * reps, ff), f32),
            pltpu.VMEM(momentum.shape, f32),
            pltpu.SemaphoreType.DMA((3,)),
        ],
        compiler_params=kernel_params(6),
        cost_estimate=pl.CostEstimate(
            flops=2 * reps * rows * momentum.size,
            bytes_accessed=8 * momentum.size + 6 * reps * rows * ff,
            transcendentals=0,
        ),
        name="final",
    )(*grams, flip, *wide, momentum)


def adasum_weights(gram):
    count = gram.shape[-1]
    index = jnp.arange(count)
    weights = jnp.ones(gram.shape[:2], f32)
    half = count // 2
    while half >= 1:
        partner = index ^ half
        square = jnp.maximum(jnp.sum(jnp.where(index[:, None] == index[None, :], gram, 0.0), 2), 0.0)
        inner = jnp.sum(jnp.where(partner[:, None] == index[None, :], gram, 0.0), 2)
        bound = jnp.sqrt(square * square[:, partner])
        inner = jnp.clip(inner, -bound, bound)
        coef = 1.0 - inner / (2.0 * (square + tiny_eps))
        weights = weights * coef
        gram = gram * coef[:, :, None] * coef[:, None, :]
        gram = gram + gram[:, partner]
        gram = gram + gram[:, :, partner]
        half //= 2
    return weights


def forward_plain(x_rows, row_cot, gate_vals, weights, sizes):
    owners, _, live, chips, width, _ = sizes
    routed = live_rows(x_rows[0], owners, live)
    out_cot = live_rows(row_cot[0], owners, live)
    gate_row = live_rows(gate_vals[0][:, None], owners, live)
    rows = routed.shape[0]
    scaled = (gate_row * out_cot.astype(f32)).astype(bf16)
    gate_pre = jnp.dot(routed, weights[0, 0], preferred_element_type=f32)
    up_pre = jnp.dot(routed, weights[0, 1], preferred_element_type=f32)
    hidden_grad = jnp.dot(scaled, weights[0, 2], preferred_element_type=f32)
    small = jnp.concatenate(backward_parts(gate_pre, up_pre, hidden_grad), axis=1)
    sides = [routed.reshape(rows, 2 * chips, width), scaled.reshape(rows, 2 * chips, width)]
    slices = jnp.concatenate(sides, axis=2).transpose(1, 0, 2)
    return slices, small


def gram_plain(lefts, rights):
    grams = []
    for left, right in zip(lefts, rights, strict=True):
        each = jnp.einsum("rnd,rnf->rdf", left, right, preferred_element_type=f32)
        grams.append(jnp.einsum("rdf,sdf->rs", each, each, precision=HIGHEST))
    return jnp.stack(grams)


def final_plain(coefs, lefts, rights, momentum):
    combined = []
    for t in range(3):
        right = (coefs[t][:, None, None] * rights[t].astype(f32)).astype(bf16)
        left = lefts[t].reshape(-1, lefts[t].shape[2])
        combined.append(
            lax.dot_general(
                left, right.reshape(-1, right.shape[2]), contract_rows, preferred_element_type=f32
            )
        )
    return moment_decay * momentum + (1.0 - moment_decay) * jnp.stack(combined)[None]


def back_plain(small, weights, sizes):
    owners, live, ff = sizes[0], sizes[2], sizes[5]
    grad = lax.dot_general(small[:, :ff], weights[0, 0], contract_cols, preferred_element_type=f32)
    grad = grad + lax.dot_general(
        small[:, ff : 2 * ff], weights[0, 1], contract_cols, preferred_element_type=f32
    )
    return grad.astype(bf16).reshape(owners, live, -1)


def token_plain(route_pos, returned, cap):
    owners, live, depth = returned.shape
    place = route_pos[0] // cap * live + route_pos[0] % cap
    picks = jnp.sum(place[:, :, None] == jnp.arange(owners * live)[None, None, :], axis=1)
    returned = returned.reshape(owners * live, depth)
    return jnp.dot(picks.astype(bf16), returned, preferred_element_type=f32).astype(bf16)[None]


def turns(blocks):
    got = [blocks[0]]
    for k in range(1, len(blocks)):
        got.append(turn_swap(blocks[k], k))
    return got


def core_swaps(blocks):
    got = []
    for mine in blocks:
        got += [mine, swap(mine, "rep", 1)]
    return [got[block] for block in block_order]


def with_kernels(x_rows, row_cot, gate_vals, route_pos, weights, momentum, sizes):
    owners, cap, _, chips, _, ff = sizes
    pairs = pack_call(x_rows, row_cot, gate_vals, sizes)
    tall = turns(pairs)
    small = forward_call(pairs, weights, sizes)
    wide = turns([small] * chips)
    returned = list(back_call(small, weights, sizes))
    for k in range(1, owners):
        returned[k] = swap(returned[k], "exp", k)
    token_grad = token_call(route_pos, returned, cap)
    tall, wide = core_swaps(tall), core_swaps(wide)
    tall_gram, flip = tall_call(tall)
    gram = gram_calls(wide, tall_gram, ff)
    gram = gram + swap(gram, "rep", 4)
    grams = [gram, swap(gram, "rep", 2)]
    return token_grad, final_call(grams, flip, wide, momentum, ff)


def without_kernels(x_rows, row_cot, gate_vals, route_pos, weights, momentum, sizes):
    _, cap, _, chips, width, ff = sizes
    reps = 2 * chips
    slices, small = forward_plain(x_rows, row_cot, gate_vals, weights, sizes)
    tall = lax.all_to_all(slices, "rep", split_axis=0, concat_axis=0, tiled=True)
    wide = [swap(small, "rep", k) if k else small for k in range(reps)]
    wide = jnp.stack(wide)
    returned = back_plain(small, weights, sizes)
    returned = lax.all_to_all(returned, "exp", split_axis=0, concat_axis=0, tiled=True)
    token_grad = token_plain(route_pos, returned, cap)
    order = jnp.arange(reps) ^ lax.axis_index("rep")
    tall = tall[order]
    lefts = [tall[:, :, :width], tall[:, :, :width], tall[:, :, width:]]
    rights = [wide[:, :, t * ff : (t + 1) * ff] for t in range(3)]
    gram = gram_plain(lefts, rights)[:, order][:, :, order]
    mask = chips
    while mask >= 1:
        gram = gram + swap(gram, "rep", mask)
        mask //= 2
    return token_grad, final_plain(adasum_weights(gram)[:, order], lefts, rights, momentum)


def on_device(x_rows, row_cot, gate_vals, route_pos, weights, momentum):
    reps = lax.axis_size("rep")
    owners = lax.axis_size("exp")
    cap = x_rows.shape[1] // owners
    live = min(cap, route_pos.shape[1])
    width = x_rows.shape[2] // reps
    ff = weights.shape[3]
    sizes = (owners, cap, live, reps // 2, width, ff)
    body = with_kernels if kernels_fit(reps, owners, live, width, ff) else without_kernels
    return body(x_rows, row_cot, gate_vals, route_pos, weights, momentum, sizes)


def kernels_fit(reps, owners, live, width, ff):
    return width % 128 == 0 and ff % 128 == 0 and owners * live % 16 == 0 and reps == 8


def solution(mesh):
    placed = (
        P("rep", "exp", None),
        P("rep", "exp", None),
        P("rep", "exp"),
        P("rep", "exp", None),
        P("exp", None, None, None),
        P("exp", None, "rep", None),
    )
    return jax.shard_map(
        on_device,
        mesh=mesh,
        in_specs=placed,
        out_specs=(P("rep", "exp", None), P("exp", None, "rep", None)),
        check_vma=False,
    )
```

```python
import functools

import jax
import jax.numpy as jnp
from jax import lax
from jax.experimental import pallas as pl
from jax.experimental.pallas import tpu as pltpu
from jax.sharding import PartitionSpec as P

tiny_eps = 1e-06
moment_decay = 0.9
HIGHEST = lax.Precision.HIGHEST
pack_flops = 10**11
bf16, f32 = jnp.bfloat16, jnp.float32
contract_rows = (((0,), (0,)), ((), ()))
contract_cols = (((1,), (1,)), ((), ()))


def swap(block, axis, mask):
    count = lax.axis_size(axis)
    return lax.ppermute(block, axis, [(i, i ^ mask) for i in range(count)])


def turn_step(core, turn):
    return turn if turn in (0, 3) else turn ^ 3 ^ (3 * core)


def turn_swap(block, turn):
    count = lax.axis_size("rep")
    route = [(i, i ^ (2 * turn_step(i & 1, turn))) for i in range(count)]
    return lax.ppermute(block, "rep", route)


block_order = (0, 1, 2, 4, 6, 3, 5, 7)
late_blocks = 3


def replica_of(me, place):
    core, block = me & 1, block_order[place]
    if block & 1:
        core, me = 1 - core, me ^ 1
    return me ^ (2 * turn_step(core, block >> 1))


def live_rows(block, owners, live):
    width = block.shape[-1]
    return block.reshape(owners, -1, width)[:, :live].reshape(owners * live, width)


def backward_parts(gate_pre, up_pre, hidden_grad):
    sigma_gate = jax.nn.sigmoid(gate_pre)
    activation = gate_pre * sigma_gate
    hidden = (activation * up_pre).astype(bf16)
    gate_grad = (hidden_grad * up_pre * sigma_gate * (1.0 + gate_pre * (1.0 - sigma_gate))).astype(
        bf16
    )
    up_grad = (hidden_grad * activation).astype(bf16)
    return gate_grad, up_grad, hidden


VMEM = pl.BlockSpec(memory_space=pltpu.VMEM)
HBM = pl.BlockSpec(memory_space=pltpu.HBM)


def in_hbm(array):
    return pltpu.with_memory_space_constraint(array, pltpu.HBM)


def kernel_params(mib):
    return pltpu.CompilerParams(vmem_limit_bytes=mib << 20)


def spread_rows(index, live, cap, owners):
    place = index
    for owner in range(1, owners):
        place = place + jnp.where(index >= owner * live, cap - live, 0)
    return place


def turn_columns(turn, width):
    me = lax.axis_index("rep")
    chip = (me >> 1) ^ turn_step(me & 1, turn)
    return pl.ds(pl.multiple_of(chip * 2 * width, 2 * width), 2 * width)


def pack(sizes, x, cot, gate, out_ref):
    owners, cap, live, _, width, _ = sizes
    slots, rows = owners * cap, owners * live
    place = spread_rows(lax.broadcasted_iota(jnp.int32, (rows, slots), 0), live, cap, owners)
    slot = lax.broadcasted_iota(jnp.int32, (rows, slots), 1)
    select = jnp.where(place == slot, 1.0, 0.0).astype(bf16)
    line = lax.broadcasted_iota(jnp.int32, (slots, slots), 0)
    lane = lax.broadcasted_iota(jnp.int32, (slots, slots), 1)
    gate = jnp.sum(jnp.where(line == lane, gate, 0.0), axis=1, keepdims=True)
    scaled = (gate * cot.astype(f32)).astype(bf16)
    routed = jnp.dot(select, x, preferred_element_type=f32).astype(bf16)
    scaled = jnp.dot(select, scaled, preferred_element_type=f32).astype(bf16)
    for core in range(2):
        out_ref[core, :, :width] = routed[:, core * width : (core + 1) * width]
        out_ref[core, :, width:] = scaled[:, core * width : (core + 1) * width]


def pack_one_kernel(sizes, x_hbm, cot_hbm, gate_hbm, out_ref, x_ref, cot_ref, gate_ref, sems):
    at = turn_columns(1, sizes[4])
    copies = [
        pltpu.make_async_copy(x_hbm.at[0, :, at], x_ref, sems.at[0]),
        pltpu.make_async_copy(cot_hbm.at[0, :, at], cot_ref, sems.at[1]),
        pltpu.make_async_copy(gate_hbm, gate_ref, sems.at[2]),
    ]
    for copy in copies:
        copy.start()
    for copy in copies:
        copy.wait()
    pack(sizes, x_ref[...], cot_ref[...], gate_ref[...], out_ref)


def pack_rest_kernel(sizes, turns, x_ref, cot_ref, gate_ref, *out_refs):
    for turn, out_ref in zip(turns, out_refs, strict=True):
        at = turn_columns(turn, sizes[4])
        pack(sizes, x_ref[0, :, at], cot_ref[0, :, at], gate_ref[...], out_ref)


def pack_one_call(x_rows, row_cot, gate_vals, sizes):
    owners, cap, live, chips, width, _ = sizes
    block = pltpu.VMEM((owners * cap, 2 * width), bf16)
    return pl.pallas_call(
        functools.partial(pack_one_kernel, sizes),
        out_shape=jax.ShapeDtypeStruct((2, owners * live, 2 * width), bf16),
        in_specs=[HBM] * 3,
        out_specs=VMEM,
        scratch_shapes=[
            block,
            block,
            pltpu.VMEM((1, owners * cap), f32),
            pltpu.SemaphoreType.DMA((3,)),
        ],
        compiler_params=kernel_params(4),
        cost_estimate=pl.CostEstimate(
            flops=pack_flops, bytes_accessed=8 * x_rows.size // chips, transcendentals=0
        ),
        name="pack_one",
    )(in_hbm(x_rows), in_hbm(row_cot), in_hbm(gate_vals))


def pack_rest_call(x_rows, row_cot, gate_vals, sizes):
    owners, _, live, chips, width, _ = sizes
    turns = [k for k in range(chips) if k != 1]
    shape = jax.ShapeDtypeStruct((2, owners * live, 2 * width), bf16)
    return pl.pallas_call(
        functools.partial(pack_rest_kernel, sizes, turns),
        out_shape=[shape] * len(turns),
        in_specs=[VMEM] * 3,
        out_specs=[VMEM] * len(turns),
        compiler_params=kernel_params(4),
        cost_estimate=pl.CostEstimate(
            flops=4 * owners * live * x_rows.size, bytes_accessed=8 * x_rows.size, transcendentals=0
        ),
        name="pack_rest",
    )(x_rows, row_cot, gate_vals)


def forward_kernel(sizes, *refs):
    _, _, _, chips, width, ff = sizes
    pair_refs, w_ref, small_ref = refs[:chips], refs[chips], refs[chips + 1]
    me = lax.axis_index("rep")
    sums = [None] * 3
    for k in range(chips):
        chip = (me >> 1) ^ turn_step(me & 1, k)
        for core in range(2):
            at = pl.ds(pl.multiple_of((chip * 2 + core) * width, width), width)
            for t in range(3):
                left = pair_refs[k][core, :, width:] if t == 2 else pair_refs[k][core, :, :width]
                part = jnp.dot(left, w_ref[0, t, at, :], preferred_element_type=f32)
                sums[t] = part if sums[t] is None else sums[t] + part
    for t, part in enumerate(backward_parts(*sums)):
        small_ref[:, t * ff : (t + 1) * ff] = part


def forward_call(pairs, weights, sizes):
    owners, _, live, chips, _, ff = sizes
    rows = owners * live
    return pl.pallas_call(
        functools.partial(forward_kernel, sizes),
        out_shape=jax.ShapeDtypeStruct((rows, 3 * ff), bf16),
        in_specs=[VMEM] * (chips + 1),
        out_specs=VMEM,
        compiler_params=kernel_params(7),
        cost_estimate=pl.CostEstimate(
            flops=2 * rows * weights.size,
            bytes_accessed=2 * weights.size,
            transcendentals=rows * ff,
        ),
        name="forward",
    )(*pairs, weights)


def back_kernel(sizes, small_ref, w_ref, *out_refs):
    owners, cap, live, chips, width, ff = sizes
    slots, rows = owners * cap, owners * live
    me = lax.axis_index("exp")
    slot = lax.broadcasted_iota(jnp.int32, (slots, rows), 0)
    row = lax.broadcasted_iota(jnp.int32, (slots, rows), 1)
    place = jnp.full((slots, rows), -1, jnp.int32)
    for k in range(owners):
        inside = (slot >= k * cap) & (slot < k * cap + live)
        place = jnp.where(inside, slot - k * cap + (me ^ k) * live, place)
    select = jnp.where(place == row, 1.0, 0.0).astype(bf16)
    spread = jnp.dot(select, small_ref[:, : 2 * ff], preferred_element_type=f32).astype(bf16)
    chunk = 2 * width
    for c in range(chips):
        at = slice(c * chunk, (c + 1) * chunk)
        grad = lax.dot_general(
            spread[:, :ff], w_ref[0, 0, at, :], contract_cols, preferred_element_type=f32
        ) + lax.dot_general(
            spread[:, ff:], w_ref[0, 1, at, :], contract_cols, preferred_element_type=f32
        )
        grad = grad.astype(bf16)
        for k in range(owners):
            out_refs[k][:, at] = grad[k * cap : k * cap + live]


def back_call(small, weights, sizes):
    owners, _, live, _, _, ff = sizes
    rows, depth = owners * live, weights.shape[2]
    return pl.pallas_call(
        functools.partial(back_kernel, sizes),
        out_shape=[jax.ShapeDtypeStruct((live, depth), bf16)] * owners,
        in_specs=[VMEM] * 2,
        out_specs=[VMEM] * owners,
        compiler_params=kernel_params(7),
        cost_estimate=pl.CostEstimate(
            flops=4 * rows * depth * ff,
            bytes_accessed=weights.size * 4 // 3,
            transcendentals=0,
        ),
        name="back",
    )(small, weights)


def token_kernel(cap, route_ref, *refs):
    row_refs, out_ref, held = refs[:-2], refs[-2], refs[-1]
    owners, live = len(row_refs), row_refs[0].shape[0]
    me = lax.axis_index("exp")
    held[...] = jnp.zeros_like(held)
    for k in range(owners):
        held[k * cap : k * cap + live] = row_refs[k][...]
    picks, tokens = route_ref.shape[1:]
    line = lax.broadcasted_iota(jnp.int32, (owners * cap, tokens), 0)
    place = line
    for k in range(owners):
        inside = (line >= k * cap) & (line < (k + 1) * cap)
        place = jnp.where(inside, line + ((me ^ k) - k) * cap, place)
    choice = jnp.zeros((owners * cap, tokens), f32)
    for pick in range(picks):
        choice = choice + jnp.where(route_ref[0, pick : pick + 1, :] == place, 1.0, 0.0)
    sums = lax.dot_general(
        choice.astype(bf16), held[...], contract_rows, preferred_element_type=f32
    )
    out_ref[0] = sums.astype(bf16)


def token_call(route_pos, returned, cap):
    owners, (live, depth) = len(returned), returned[0].shape
    return pl.pallas_call(
        functools.partial(token_kernel, cap),
        out_shape=jax.ShapeDtypeStruct((1, route_pos.shape[1], depth), bf16),
        in_specs=[VMEM] * (owners + 1),
        out_specs=VMEM,
        scratch_shapes=[pltpu.VMEM((owners * cap, depth), bf16)],
        compiler_params=kernel_params(6),
        cost_estimate=pl.CostEstimate(
            flops=2 * route_pos.shape[1] * owners * cap * depth,
            bytes_accessed=owners * live * depth * 4,
            transcendentals=0,
        ),
        name="token",
    )(route_pos.swapaxes(1, 2), *returned)


def tall_kernel(start, *refs):
    tall_refs, gram_ref, flip_ref = refs[:-2], refs[-2], refs[-1]
    rows, width = tall_refs[0].shape[1], tall_refs[0].shape[2] // 2
    core = lax.axis_index("rep") & 1
    for side in range(2):
        at = slice(side * width, (side + 1) * width)
        both = jnp.concatenate(
            [jnp.concatenate([ref[0, :, at], ref[1, :, at]], axis=1) for ref in tall_refs], axis=0
        )
        gram_ref[side] = lax.dot_general(
            both[start * rows :], both, contract_cols, preferred_element_type=f32
        )
        own = jnp.concatenate([ref[core, :, at] for ref in tall_refs[start:]], axis=0)
        flip_ref[side] = own.T


def tall_call(tall, start):
    blocks, (cores, rows, width) = len(tall), tall[0].shape
    width //= 2
    flat, most = blocks * rows, (blocks - start) * rows
    return pl.pallas_call(
        functools.partial(tall_kernel, start),
        out_shape=[
            jax.ShapeDtypeStruct((2, most, flat), f32),
            jax.ShapeDtypeStruct((2, width, most), bf16),
        ],
        in_specs=[VMEM] * blocks,
        out_specs=[VMEM] * 2,
        compiler_params=kernel_params(6),
        cost_estimate=pl.CostEstimate(
            flops=8 * flat * most * width,
            bytes_accessed=8 * flat * most + 12 * flat * width,
            transcendentals=0,
        ),
    )(*tall)


def pair_sums(wide_refs, tall_ref, ff, me, start):
    reps, rows = len(wide_refs), wide_refs[0].shape[0]
    flat = reps * rows
    spot = lax.broadcasted_iota(jnp.int32, (flat, 128), 0)
    lane = lax.broadcasted_iota(jnp.int32, (flat, 128), 1)
    group = jnp.full_like(spot, me)
    for k in range(1, reps):
        group = jnp.where(spot >= k * rows, replica_of(me, k), group)
    gather = jnp.where(group == (lane & 7), 1.0, 0.0)
    sums = []
    for t in range(3):
        block = jnp.concatenate([ref[:, t * ff : (t + 1) * ff] for ref in wide_refs], axis=0)
        both = lax.dot_general(
            block[start * rows :], block, contract_cols, preferred_element_type=f32
        )
        both = both * tall_ref[t // 2]
        both = both.reshape(reps - start, rows // 8, 8, flat)
        sums.append(jnp.sum(both, axis=1).reshape((reps - start) * 8, flat))
    sums = jnp.dot(
        jnp.concatenate(sums, axis=0), gather, precision=HIGHEST, preferred_element_type=f32
    )
    return jnp.sum(sums.reshape(3 * (reps - start), 8, 128), axis=1)


def first_kernel(reps, ff, *refs):
    wide_refs, tall_ref, out_ref = refs[:-2], refs[-2], refs[-1]
    me, count = lax.axis_index("rep"), len(wide_refs)
    sums = pair_sums(wide_refs, tall_ref, ff, me, 0)
    out_ref[...] = jnp.zeros_like(out_ref)
    for t in range(3):
        for k in range(count):
            at = pl.ds(t * reps + replica_of(me, k), 1)
            out_ref[at, :] = sums[t * count + k : t * count + k + 1]


def last_kernel(reps, ff, *refs):
    wide_refs, tall_ref, first_ref, out_ref = refs[:reps], refs[reps], refs[reps + 1], refs[reps + 2]
    me = lax.axis_index("rep")
    sums = pair_sums(wide_refs, tall_ref, ff, me, reps - late_blocks)
    line = lax.broadcasted_iota(jnp.int32, (reps, 128), 0)
    lane = lax.broadcasted_iota(jnp.int32, (reps, 128), 1)
    near = lane & (reps - 1)
    owns = [replica_of(me, k) for k in range(reps - late_blocks, reps)]
    old = line >= 0
    for own in owns:
        old = old & (line != own)
    for t in range(3):
        gram = first_ref[t * reps : (t + 1) * reps, :]
        for j, own in enumerate(owns):
            row = jnp.broadcast_to(sums[late_blocks * t + j : late_blocks * t + j + 1], (reps, 128))
            column = jnp.sum(jnp.where(line == lane, row, 0.0), axis=1, keepdims=True)
            gram = gram + jnp.where(line == own, row, 0.0)
            gram = gram + jnp.where(old & (near == own), column, 0.0)
        out_ref[t * reps : (t + 1) * reps, :] = gram


def gram_calls(wide, first_tall, last_tall, ff):
    reps, rows = len(wide), wide[0].shape[0]
    flat = reps * rows
    shape = jax.ShapeDtypeStruct((3 * reps, 128), f32)
    first = pl.pallas_call(
        functools.partial(first_kernel, reps, ff),
        out_shape=shape,
        in_specs=[VMEM] * (reps - late_blocks + 1),
        out_specs=VMEM,
        compiler_params=kernel_params(6),
        cost_estimate=pl.CostEstimate(
            flops=3 * flat * flat * ff,
            bytes_accessed=4 * flat * flat + 4 * flat * ff,
            transcendentals=0,
        ),
        name="first",
    )(*wide[:-late_blocks], first_tall)
    return pl.pallas_call(
        functools.partial(last_kernel, reps, ff),
        out_shape=shape,
        in_specs=[VMEM] * (reps + 2),
        out_specs=VMEM,
        compiler_params=kernel_params(6),
        cost_estimate=pl.CostEstimate(
            flops=3 * flat * flat * ff // 2,
            bytes_accessed=2 * flat * flat + 6 * flat * ff,
            transcendentals=0,
        ),
        name="last",
    )(*wide, last_tall, first)


def final_kernel(reps, ff, *refs):
    gram_refs, flip_refs, refs = refs[:2], refs[2:4], refs[4:]
    wide_refs, (moment_ref, out_hbm, coef_ref, out_ref, sems) = refs[:reps], refs[reps:]
    copies = []
    me = lax.axis_index("rep")
    line = lax.broadcasted_iota(jnp.int32, (reps, 128), 0)
    lane = lax.broadcasted_iota(jnp.int32, (reps, 128), 1)
    near = lane & (reps - 1)
    for t in range(3):
        part = slice(t * reps, (t + 1) * reps)
        gram = gram_refs[0][part, :] + gram_refs[1][part, :]
        coefs = jnp.ones((reps, 128), f32)
        half = reps // 2
        while half >= 1:

            def factor(axis, spot):
                square = jnp.where(spot == line, gram, 0.0)
                square = jnp.maximum(jnp.sum(square, axis=axis, keepdims=True), 0.0)
                square = jnp.broadcast_to(square, (reps, 128))
                inner = jnp.where(spot == line ^ half, gram, 0.0)
                inner = jnp.sum(inner, axis=axis, keepdims=True)
                bound = jnp.sqrt(square * pltpu.roll(square, half, 1 - axis))
                inner = jnp.clip(inner, -bound, bound)
                return 1.0 - inner / (2.0 * (square + tiny_eps))

            by_line, by_lane = factor(1, lane), factor(0, near)
            coefs = coefs * by_line
            gram = gram * by_line * by_lane
            gram = gram + pltpu.roll(gram, half, 0)
            gram = gram + pltpu.roll(gram, half, 1)
            half //= 2
        coef_ref[part, :] = jnp.concatenate([coefs] * (ff // 128), axis=1)
    for t in range(3):
        scaled = []
        for k in range(reps):
            coef = coef_ref[pl.ds(t * reps + replica_of(me, k), 1), :]
            scaled.append((coef * wide_refs[k][:, t * ff : (t + 1) * ff].astype(f32)).astype(bf16))
        combined = 0.0
        for flip_ref, part in zip(flip_refs, (scaled[:-late_blocks], scaled[-late_blocks:])):
            part = jnp.concatenate(part, axis=0)
            combined += jnp.dot(flip_ref[t // 2], part, preferred_element_type=f32)
        out_ref[0, t] = moment_decay * moment_ref[0, t] + (1.0 - moment_decay) * combined
        copies.append(pltpu.make_async_copy(out_ref.at[0, t], out_hbm.at[0, t], sems.at[t]))
        copies[t].start()
    for copy in copies:
        copy.wait()


def final_call(grams, flips, wide, momentum, ff):
    reps, rows = len(wide), wide[0].shape[0]
    return pl.pallas_call(
        functools.partial(final_kernel, reps, ff),
        out_shape=jax.ShapeDtypeStruct(momentum.shape, f32),
        in_specs=[VMEM] * (len(grams) + len(flips) + reps + 1),
        out_specs=HBM,
        scratch_shapes=[
            pltpu.VMEM((3 * reps, ff), f32),
            pltpu.VMEM(momentum.shape, f32),
            pltpu.SemaphoreType.DMA((3,)),
        ],
        compiler_params=kernel_params(6),
        cost_estimate=pl.CostEstimate(
            flops=2 * reps * rows * momentum.size,
            bytes_accessed=8 * momentum.size + 6 * reps * rows * ff,
            transcendentals=0,
        ),
        name="final",
    )(*grams, *flips, *wide, momentum)


def adasum_weights(gram):
    count = gram.shape[-1]
    index = jnp.arange(count)
    weights = jnp.ones(gram.shape[:2], f32)
    half = count // 2
    while half >= 1:
        partner = index ^ half
        square = jnp.maximum(jnp.sum(jnp.where(index[:, None] == index[None, :], gram, 0.0), 2), 0.0)
        inner = jnp.sum(jnp.where(partner[:, None] == index[None, :], gram, 0.0), 2)
        bound = jnp.sqrt(square * square[:, partner])
        inner = jnp.clip(inner, -bound, bound)
        coef = 1.0 - inner / (2.0 * (square + tiny_eps))
        weights = weights * coef
        gram = gram * coef[:, :, None] * coef[:, None, :]
        gram = gram + gram[:, partner]
        gram = gram + gram[:, :, partner]
        half //= 2
    return weights


def forward_plain(x_rows, row_cot, gate_vals, weights, sizes):
    owners, _, live, chips, width, _ = sizes
    routed = live_rows(x_rows[0], owners, live)
    out_cot = live_rows(row_cot[0], owners, live)
    gate_row = live_rows(gate_vals[0][:, None], owners, live)
    rows = routed.shape[0]
    scaled = (gate_row * out_cot.astype(f32)).astype(bf16)
    gate_pre = jnp.dot(routed, weights[0, 0], preferred_element_type=f32)
    up_pre = jnp.dot(routed, weights[0, 1], preferred_element_type=f32)
    hidden_grad = jnp.dot(scaled, weights[0, 2], preferred_element_type=f32)
    small = jnp.concatenate(backward_parts(gate_pre, up_pre, hidden_grad), axis=1)
    sides = [routed.reshape(rows, 2 * chips, width), scaled.reshape(rows, 2 * chips, width)]
    slices = jnp.concatenate(sides, axis=2).transpose(1, 0, 2)
    return slices, small


def gram_plain(lefts, rights):
    grams = []
    for left, right in zip(lefts, rights, strict=True):
        each = jnp.einsum("rnd,rnf->rdf", left, right, preferred_element_type=f32)
        grams.append(jnp.einsum("rdf,sdf->rs", each, each, precision=HIGHEST))
    return jnp.stack(grams)


def final_plain(coefs, lefts, rights, momentum):
    combined = []
    for t in range(3):
        right = (coefs[t][:, None, None] * rights[t].astype(f32)).astype(bf16)
        left = lefts[t].reshape(-1, lefts[t].shape[2])
        combined.append(
            lax.dot_general(
                left, right.reshape(-1, right.shape[2]), contract_rows, preferred_element_type=f32
            )
        )
    return moment_decay * momentum + (1.0 - moment_decay) * jnp.stack(combined)[None]


def back_plain(small, weights, sizes):
    owners, live, ff = sizes[0], sizes[2], sizes[5]
    grad = lax.dot_general(small[:, :ff], weights[0, 0], contract_cols, preferred_element_type=f32)
    grad = grad + lax.dot_general(
        small[:, ff : 2 * ff], weights[0, 1], contract_cols, preferred_element_type=f32
    )
    return grad.astype(bf16).reshape(owners, live, -1)


def token_plain(route_pos, returned, cap):
    owners, live, depth = returned.shape
    place = route_pos[0] // cap * live + route_pos[0] % cap
    picks = jnp.sum(place[:, :, None] == jnp.arange(owners * live)[None, None, :], axis=1)
    returned = returned.reshape(owners * live, depth)
    return jnp.dot(picks.astype(bf16), returned, preferred_element_type=f32).astype(bf16)[None]


def turns(blocks):
    got = [blocks[0]]
    for k in range(1, len(blocks)):
        got.append(turn_swap(blocks[k], k))
    return got


def core_swaps(blocks):
    got = []
    for mine in blocks:
        got += [mine, swap(mine, "rep", 1)]
    return [got[block] for block in block_order]


def with_kernels(x_rows, row_cot, gate_vals, route_pos, weights, momentum, sizes):
    owners, cap, _, chips, _, ff = sizes
    pair = pack_one_call(x_rows, row_cot, gate_vals, sizes)
    pairs = pack_rest_call(x_rows, row_cot, gate_vals, sizes)
    pairs = [pairs[0], pair, *pairs[1:]]
    tall = turns(pairs)
    small = forward_call(pairs, weights, sizes)
    wide = turns([small] * chips)
    returned = list(back_call(small, weights, sizes))
    for k in range(1, owners):
        returned[k] = swap(returned[k], "exp", k)
    token_grad = token_call(route_pos, returned, cap)
    tall, wide = core_swaps(tall), core_swaps(wide)
    start = len(tall) - late_blocks
    first_tall, first_flip = tall_call(tall[:start], 0)
    last_tall, last_flip = tall_call(tall, start)
    gram = gram_calls(wide, first_tall, last_tall, ff)
    gram = gram + swap(gram, "rep", 4)
    grams = [gram, swap(gram, "rep", 2)]
    return token_grad, final_call(grams, [first_flip, last_flip], wide, momentum, ff)


def without_kernels(x_rows, row_cot, gate_vals, route_pos, weights, momentum, sizes):
    _, cap, _, chips, width, ff = sizes
    reps = 2 * chips
    slices, small = forward_plain(x_rows, row_cot, gate_vals, weights, sizes)
    tall = lax.all_to_all(slices, "rep", split_axis=0, concat_axis=0, tiled=True)
    wide = [swap(small, "rep", k) if k else small for k in range(reps)]
    wide = jnp.stack(wide)
    returned = back_plain(small, weights, sizes)
    returned = lax.all_to_all(returned, "exp", split_axis=0, concat_axis=0, tiled=True)
    token_grad = token_plain(route_pos, returned, cap)
    order = jnp.arange(reps) ^ lax.axis_index("rep")
    tall = tall[order]
    lefts = [tall[:, :, :width], tall[:, :, :width], tall[:, :, width:]]
    rights = [wide[:, :, t * ff : (t + 1) * ff] for t in range(3)]
    gram = gram_plain(lefts, rights)[:, order][:, :, order]
    mask = chips
    while mask >= 1:
        gram = gram + swap(gram, "rep", mask)
        mask //= 2
    return token_grad, final_plain(adasum_weights(gram)[:, order], lefts, rights, momentum)


def on_device(x_rows, row_cot, gate_vals, route_pos, weights, momentum):
    reps = lax.axis_size("rep")
    owners = lax.axis_size("exp")
    cap = x_rows.shape[1] // owners
    live = min(cap, route_pos.shape[1])
    width = x_rows.shape[2] // reps
    ff = weights.shape[3]
    sizes = (owners, cap, live, reps // 2, width, ff)
    body = with_kernels if kernels_fit(reps, owners, live, width, ff) else without_kernels
    return body(x_rows, row_cot, gate_vals, route_pos, weights, momentum, sizes)


def kernels_fit(reps, owners, live, width, ff):
    return width % 128 == 0 and ff % 128 == 0 and owners * live % 16 == 0 and reps == 8


def solution(mesh):
    placed = (
        P("rep", "exp", None),
        P("rep", "exp", None),
        P("rep", "exp"),
        P("rep", "exp", None),
        P("exp", None, None, None),
        P("exp", None, "rep", None),
    )
    return jax.shard_map(
        on_device,
        mesh=mesh,
        in_specs=placed,
        out_specs=(P("rep", "exp", None), P("exp", None, "rep", None)),
        check_vma=False,
    )
```
